128 devices in a mesh: band: 8 (over z_hi, y), blk: 16 (over x, z_lo, core).
Axes of the slice: x: 4, y: 4, z: 4 (z_hi: 2, z_lo: 2; z = z_hi * 2 + z_lo), core: 2. Of those that a mesh axis runs over, the one named last changes fastest.
Arguments:
- volt: bfloat16 [2, 2048, 110592], P(None, ('blk', 'band')), may hold values from -6 to 6
- band_chans: int32 [8, 8], replicated, may hold values from 0 to 4095, as said below
- band_count: int32 [8], replicated, may hold values from 1 to 8, as said below
Outputs:
- visibility: bfloat16 [2, 8, 8, 2048, 2048], P(None, 'band', None, 'blk')
The draws below stay inside these ranges and needn't reach their ends.
Inputs may be any that keep to these rules, and one draw needn't show every extreme that they name: `band_chans`: all entries are distinct channels; slots at or beyond a band group's count name channels too and are not correlated. `band_count`: one band group has exactly 8 live slots in every draw.
All inputs are finite; a program needn't handle non-finite values.
Results may differ from the reference program's by a relative error of at most 0.0057.
Values may be sent and summed in bfloat16 or wider, within the bound.
A program may use at most 192 MiB of HBM per device.

```python
import math
import jax
import jax.numpy as jnp
from jax import lax

E = 2048
C = 4096
TAPS = 16
NSPEC = 12
CSLOT = 8
NF = 27
SAMPLES = 110592
N_BAND = 8


def draw_band_chans(key, part):
    shuffled = jax.random.permutation(jax.random.fold_in(key, 11), C)
    return shuffled[:N_BAND * CSLOT].reshape(N_BAND, CSLOT).astype(jnp.int32)


def draw_band_count(key, part):
    counts = jax.random.randint(jax.random.fold_in(key, 21), (N_BAND,), 1, CSLOT + 1)
    fullest = jax.random.randint(jax.random.fold_in(key, 22), (), 0, N_BAND)
    positions = jnp.arange(N_BAND, dtype=jnp.int32)
    return jnp.where(positions == fullest, CSLOT, counts).astype(jnp.int32)


def levels(own_key, dims, pieces, low, top_value):
    factor_of, own = 1.0, jax.random.fold_in(own_key, 6)
    for position, blocks in pieces:
        steps = jnp.exp(jax.random.uniform(jax.random.fold_in(own, position), (blocks,), jnp.float32, low / len(pieces), top_value / len(pieces)))
        factor_of = factor_of * jnp.repeat(steps, dims[position] // blocks).reshape([-1 if axis == position else 1 for axis in range(len(dims))])
    return factor_of


def noise(stream_key, shape, scale, bound, shards=(), held_as=jnp.bfloat16):
    drawn = scale * jax.random.normal(stream_key, shape, jnp.float32)
    if shards:
        drawn = drawn * levels(stream_key, shape, shards, -0.22, 0.18)
    return jnp.clip(drawn, -bound, bound).astype(held_as)


def setup_inputs(seed: int = 0) -> dict:
    splits = jax.random.split(jax.random.key(seed), 4)
    volt = noise(splits[0], (2, E, SAMPLES), 1.0, 6.0, ((1, 128),))
    band_chans = draw_band_chans(jax.random.fold_in(splits[3], 71), 0)
    band_count = draw_band_count(jax.random.fold_in(splits[3], 71), 0)
    return dict(volt=volt, band_chans=band_chans, band_count=band_count)


def taper_table(taps, width):
    sample_idx = jnp.arange(taps * width, dtype=jnp.float32)
    centre = (sample_idx + 0.5) / width - taps / 2.0
    window = 0.5 - 0.5 * jnp.cos(2.0 * math.pi * (sample_idx + 0.5) / (taps * width))
    prototype = jnp.sinc(centre) * window
    prototype = prototype / jnp.sqrt(jnp.sum(prototype * prototype))
    return prototype.reshape(taps, width)

def reference(volt, band_chans, band_count):
    taper = taper_table(TAPS, C)
    channels = band_chans.reshape(-1).astype(jnp.int32)
    blocks = jnp.moveaxis(volt.reshape(2, E // 128, 128, SAMPLES), 1, 0)

    def front_end(element_block):
        samples = element_block.astype(jnp.float32).reshape(2, 128, NF, C)
        weighted = taper[0] * samples[:, :, 0:NSPEC, :]
        for tap_idx in range(1, TAPS):
            weighted = weighted + taper[tap_idx] * samples[:, :, tap_idx:tap_idx + NSPEC, :]
        complex_spec = jnp.fft.fft(weighted[0] + 1j * weighted[1], axis=-1)
        picked = jnp.take(complex_spec, channels, axis=-1)
        return jnp.stack([jnp.real(picked), jnp.imag(picked)]).astype(jnp.bfloat16)
    spectra = lax.map(front_end, blocks)
    spectra = jnp.moveaxis(spectra, 0, 1).reshape(2, E, NSPEC, N_BAND, CSLOT)
    spectra = spectra.astype(jnp.float32)
    live_mask = (jnp.arange(CSLOT, dtype=jnp.int32)[None, :] < band_count[:, None]).astype(jnp.float32)

    def band_vis(pair):
        band_spectra, band_live = pair
        spec_real = band_spectra[0] * band_live
        spec_imag = band_spectra[1] * band_live
        real_part = jnp.einsum('its,jts->sij', spec_real, spec_real) + jnp.einsum('its,jts->sij', spec_imag, spec_imag)
        imag_part = jnp.einsum('its,jts->sij', spec_imag, spec_real) - jnp.einsum('its,jts->sij', spec_real, spec_imag)
        return (jnp.stack([real_part, imag_part]) / NSPEC).astype(jnp.bfloat16)
    result = lax.map(band_vis, (jnp.moveaxis(spectra, 3, 0), live_mask))
    return jnp.moveaxis(result, 0, 1)
```

```python
import math

import jax
import jax.numpy as jnp
import numpy as np
from jax import lax
from jax.experimental import pallas as pl
from jax.experimental.pallas import tpu as pltpu
from jax.sharding import PartitionSpec as P

C = 4096
TAPS = 16
NSPEC = 12
FRAMES = NSPEC + TAPS - 1
EL = 16
LANES = 128
BANDS = 8
SLOTS = 8
GROUPS = 4
GROUP_W = C // GROUPS
CHUNK = 256
N_CHUNK = C // CHUNK
MESH = pl.DeviceIdType.MESH
F32, BF16 = jnp.float32, jnp.bfloat16


def taper_table():
    idx = np.arange(TAPS * C, dtype=np.float64)
    centre = (idx + 0.5) / C - TAPS / 2.0
    window = 0.5 - 0.5 * np.cos(2.0 * math.pi * (idx + 0.5) / (TAPS * C))
    prototype = np.sinc(centre) * window
    prototype = prototype / np.sqrt(np.sum(prototype * prototype))
    return prototype.reshape(TAPS, C).astype(np.float32)


def cos_sin(turns):
    shifted = turns + 512
    quarter = (shifted >> 10) & 3
    x = ((shifted & 1023) - 512).astype(F32) * (2.0 * math.pi / 4096.0)
    x2 = x * x
    s = x * (1.0 + x2 * (-1.0 / 6 + x2 * (1.0 / 120 + x2 * (-1.0 / 5040 + x2 * (1.0 / 362880)))))
    c = 1.0 + x2 * (-0.5 + x2 * (1.0 / 24 + x2 * (-1.0 / 720 + x2 * (1.0 / 40320))))
    odd = (quarter & 1) == 1
    cc, ss = jnp.where(odd, s, c), jnp.where(odd, c, s)
    cc = jnp.where((quarter == 1) | (quarter == 2), -cc, cc)
    ss = jnp.where(quarter >= 2, -ss, ss)
    return cc, ss


def split(y):
    hi = y.astype(BF16)
    return hi, (y - hi.astype(F32)).astype(BF16)


def front_kernel(
    volt, chans, taper, z, samples, base_c, base_s, step_c, step_s, table, lhs_a, lhs_b, total, sems
):
    def fetch(group, frame):
        return pltpu.make_async_copy(
            volt.at[:, :, pl.ds(frame * C + group * GROUP_W, GROUP_W)],
            samples.at[group, frame],
            sems.at[group],
        )

    for group in range(GROUPS):
        for frame in range(FRAMES):
            fetch(group, frame).start()

    lane = lax.broadcasted_iota(jnp.int32, (8, LANES), 1)
    key = ((lane >> 4) << 3) + (lane & 7)
    row = jnp.zeros((8, LANES), jnp.int32)
    for g in range(BANDS):
        for s in range(SLOTS):
            row = jnp.where(key == g * SLOTS + s, chans[g, s], row)
    quarter_turn = ((lane[:1] >> 3) & 1) * 1024
    row = row[:1]
    inner = lax.broadcasted_iota(jnp.int32, (LANES, LANES), 0)
    c0, s0 = cos_sin((inner * row + quarter_turn) & 4095)
    base_c[...] = c0
    base_s[...] = s0
    outer = lax.broadcasted_iota(jnp.int32, (C // LANES, LANES), 0) * LANES
    c1, s1 = cos_sin((outer * row) & 4095)
    step_c[...] = c1
    step_s[...] = s1

    def build(chunk, carry):
        for part in range(CHUNK // LANES):
            a = chunk * (CHUNK // LANES) + part
            ca, sa = step_c[pl.ds(a, 1), :], step_s[pl.ds(a, 1), :]
            cb, sb = base_c[...], base_s[...]
            for comp, value in ((0, ca * cb - sa * sb), (1, sa * cb + ca * sb)):
                hi, lo = split(value)
                rows = slice(comp * CHUNK + part * LANES, comp * CHUNK + (part + 1) * LANES)
                table[chunk, rows, :LANES] = hi
                table[chunk, rows, LANES:] = lo
        return carry

    lax.fori_loop(0, N_CHUNK, build, 0)

    def weigh(chunk, lhs):
        group = chunk // (GROUP_W // CHUNK)
        for part in range(CHUNK // LANES):
            k = pl.multiple_of(chunk * CHUNK + part * LANES, LANES)
            in_group = pl.multiple_of(k - group * GROUP_W, LANES)
            taps = [
                jnp.broadcast_to(taper[p : p + 1, pl.ds(k, LANES)], (EL, LANES))
                for p in range(TAPS)
            ]
            for comp in range(2):
                column = slice(comp * CHUNK + part * LANES, comp * CHUNK + (part + 1) * LANES)
                acc = [None] * NSPEC
                for f in range(FRAMES):
                    x = samples[group, f, comp, :, pl.ds(in_group, LANES)].astype(F32)
                    for t in range(max(0, f - TAPS + 1), min(NSPEC - 1, f) + 1):
                        term = taps[f - t] * x
                        acc[t] = term if acc[t] is None else acc[t] + term
                    if f >= TAPS - 1:
                        t = f - TAPS + 1
                        hi, lo = split(acc[t])
                        lhs[t * EL : (t + 1) * EL, column] = hi
                        lhs[NSPEC * EL + t * EL : NSPEC * EL + (t + 1) * EL, column] = lo
                        acc[t] = None

    def transform(chunk, lhs):
        total[...] += jnp.dot(lhs[...], table[chunk], preferred_element_type=F32)

    def wait_group(group):
        pltpu.make_async_copy(samples.at[group], samples.at[group], sems.at[group]).wait()

    total[...] = jnp.zeros_like(total)
    lhs_b[...] = jnp.zeros_like(lhs_b)

    per_group = GROUP_W // CHUNK

    def two_chunks(i, carry):
        first = i * 2
        weigh(first, lhs_a)
        transform(lax.max(first - 1, 0), lhs_b)
        weigh(first + 1, lhs_b)
        transform(first, lhs_a)
        return carry

    for group in range(GROUPS):
        wait_group(group)
        lax.fori_loop(group * per_group // 2, (group + 1) * per_group // 2, two_chunks, 0)
    transform(N_CHUNK - 1, lhs_b)

    rows = NSPEC * EL
    y = (total[:rows, LANES:] + total[rows:, :LANES]) + (
        total[rows:, LANES:] + total[:rows, :LANES]
    )
    place = lax.broadcasted_iota(jnp.int32, (EL, LANES), 1) >> 4
    for g in range(BANDS):
        for tile in range(2):
            out = jnp.zeros((EL, LANES), F32)
            for t in range(tile * 8, min(tile * 8 + 8, NSPEC)):
                moved = y[t * EL : (t + 1) * EL]
                shift = (t - g) * 16 % LANES
                if shift:
                    moved = pltpu.roll(moved, shift, 1)
                out = jnp.where(place == t - tile * 8, moved, out)
            z[g, :, tile * LANES : (tile + 1) * LANES] = out.astype(BF16)


def front(volt, chans):
    vmem = pl.BlockSpec(memory_space=pltpu.VMEM)
    return pl.pallas_call(
        front_kernel,
        out_shape=jax.ShapeDtypeStruct((BANDS, EL, 2 * LANES), BF16),
        in_specs=[
            pl.BlockSpec(memory_space=pl.ANY),
            pl.BlockSpec(memory_space=pltpu.SMEM),
            vmem,
        ],
        out_specs=vmem,
        scratch_shapes=[
            pltpu.VMEM((GROUPS, FRAMES, 2, EL, GROUP_W), BF16),
            pltpu.VMEM((LANES, LANES), F32),
            pltpu.VMEM((LANES, LANES), F32),
            pltpu.VMEM((C // LANES, LANES), F32),
            pltpu.VMEM((C // LANES, LANES), F32),
            pltpu.VMEM((N_CHUNK, 2 * CHUNK, 2 * LANES), BF16),
            pltpu.VMEM((2 * NSPEC * EL, 2 * CHUNK), BF16),
            pltpu.VMEM((2 * NSPEC * EL, 2 * CHUNK), BF16),
            pltpu.VMEM((2 * NSPEC * EL, 2 * LANES), F32),
            pltpu.SemaphoreType.DMA((GROUPS,)),
        ],
        compiler_params=pltpu.CompilerParams(vmem_limit_bytes=48 * 2**20),
        name="filterbank",
    )(volt, chans, jnp.asarray(taper_table()))


def share_kernel(
    n_band, n_blk, z, x, own, ct_send, ct_recv, ag_send, ag_recv, fw_send, fw_recv, here
):
    g, b = lax.axis_index("band"), lax.axis_index("blk")
    core, near, along = b % 2, b // 2 % 2, b // 4
    n_along = n_blk // 4
    sibling = b + 1 - 2 * core
    el = z.shape[1]
    block = el * n_band

    def chip(d_along, d_near):
        return ((along + d_along) % n_along * 2 + (near + d_near) % 2) * 2 + core

    hops = [(da, dn) for da in range(n_along) for dn in range(2) if (da, dn) != (0, 0)]
    barrier = pltpu.get_barrier_semaphore()
    peers = [((g + d) % n_band, b) for d in range(1, n_band)]
    peers += [(g, chip(*hop)) for hop in hops] + [(g, sibling)]
    for peer in peers:
        pl.semaphore_signal(barrier, inc=1, device_id=peer, device_id_type=MESH)
    pl.semaphore_wait(barrier, len(peers))

    mine = pl.ds(pl.multiple_of(g * el, el), el)
    turns = []
    for d in range(1, n_band):
        to = (g + d) % n_band
        turns.append(
            pltpu.make_async_remote_copy(
                z.at[to], own.at[mine], ct_send.at[d], ct_recv.at[d], (to, b), MESH
            )
        )
        turns[-1].start()
    keep = pltpu.make_async_copy(z.at[g], own.at[mine], here.at[0])
    keep.start()
    keep.wait()
    for turn in turns:
        turn.wait()

    def rows(owner):
        return pl.ds(pl.multiple_of(owner * block, block), block)

    sends = []
    for n, hop in enumerate(hops):
        sends.append(
            pltpu.make_async_remote_copy(
                own, x.at[rows(b)], ag_send.at[n], ag_recv.at[n], (g, chip(*hop)), MESH
            )
        )
        sends[-1].start()
    last = len(hops)
    passed = [
        pltpu.make_async_remote_copy(
            own, x.at[rows(b)], fw_send.at[last], fw_recv.at[last], (g, sibling), MESH
        )
    ]
    passed[0].start()
    keep = pltpu.make_async_copy(own, x.at[rows(b)], here.at[1])
    keep.start()
    for n, (da, dn) in enumerate(hops):
        sends[n].wait_recv()
        owner = chip(n_along - da, 2 - dn)
        passed.append(
            pltpu.make_async_remote_copy(
                x.at[rows(owner)],
                x.at[rows(owner)],
                fw_send.at[n],
                fw_recv.at[n],
                (g, sibling),
                MESH,
            )
        )
        passed[-1].start()
    keep.wait()
    for send in sends:
        send.wait_send()
    for one in passed:
        one.wait()


def share(z, n_band, n_blk):
    el, width = z.shape[1], z.shape[2]
    vmem = pl.BlockSpec(memory_space=pltpu.VMEM)
    dma = pltpu.SemaphoreType.DMA

    def body(*refs):
        share_kernel(n_band, n_blk, *refs)

    return pl.pallas_call(
        body,
        out_shape=jax.ShapeDtypeStruct((el * n_band * n_blk, width), BF16),
        in_specs=[vmem],
        out_specs=vmem,
        scratch_shapes=[
            pltpu.VMEM((el * n_band, width), BF16),
            dma((n_band,)),
            dma((n_band,)),
            dma((n_blk // 2,)),
            dma((n_blk // 2,)),
            dma((n_blk // 2,)),
            dma((n_blk // 2,)),
            dma((2,)),
        ],
        compiler_params=pltpu.CompilerParams(collective_id=0, has_side_effects=True),
        name="corner_turn_and_gather",
    )(z)


COLUMNS = 256


def correlate_kernel(x, count, out, lhs):
    j = pl.program_id(0)
    block = out.shape[3]

    @pl.when(j == 0)
    def _():
        b = lax.axis_index("blk")
        live = count[lax.axis_index("band")]
        lane = lax.broadcasted_iota(jnp.int32, (block, LANES), 1)
        slot = lane & 7
        is_real = (lane & 8) == 0
        for tile in range(2):
            cols = slice(tile * LANES, (tile + 1) * LANES)
            own = x[pl.ds(pl.multiple_of(b * block, block), block), cols].astype(F32)
            turned = jnp.where(
                is_real, pltpu.roll(own, LANES - 8, 1), -pltpu.roll(own, 8, 1)
            )
            own = jnp.where(slot < live, own, 0.0)
            turned = jnp.where(slot < live, turned, 0.0)
            if tile == 1:
                used = lane < (NSPEC - 8) * 16
                own, turned = jnp.where(used, own, 0.0), jnp.where(used, turned, 0.0)
            for s in range(SLOTS):
                for part, value in ((0, own), (1, turned)):
                    at = (part * SLOTS + s) * block
                    lhs[at : at + block, cols] = jnp.where(slot == s, value, 0.0).astype(BF16)

    right = x[pl.ds(pl.multiple_of(j * COLUMNS, COLUMNS), COLUMNS), :]
    for part in range(2):
        for s in range(SLOTS):
            at = (part * SLOTS + s) * block
            y = lax.dot_general(
                lhs[at : at + block, :], right, (((1,), (1,)), ((), ())), preferred_element_type=F32
            )
            out[part, 0, s] = (y * (1.0 / NSPEC)).astype(BF16)


def correlate(x, count, n_band, n_blk):
    everyone = x.shape[0]
    block = everyone // n_blk
    return pl.pallas_call(
        correlate_kernel,
        grid=(everyone // COLUMNS,),
        out_shape=jax.ShapeDtypeStruct((2, 1, SLOTS, block, everyone), BF16),
        in_specs=[
            pl.BlockSpec(memory_space=pltpu.VMEM),
            pl.BlockSpec(memory_space=pltpu.SMEM),
        ],
        out_specs=pl.BlockSpec((2, 1, SLOTS, block, COLUMNS), lambda j: (0, 0, 0, 0, j)),
        scratch_shapes=[pltpu.VMEM((2 * SLOTS * block, x.shape[1]), BF16)],
        compiler_params=pltpu.CompilerParams(vmem_limit_bytes=32 * 2**20),
        name="correlate",
    )(x, count)


def solution(mesh):
    n_band, n_blk = mesh.shape["band"], mesh.shape["blk"]

    def local(volt, band_chans, band_count):
        z = front(volt, band_chans)
        x = share(z, n_band, n_blk)
        return correlate(x, band_count, n_band, n_blk)

    return jax.shard_map(
        local,
        mesh=mesh,
        in_specs=(P(None, ("blk", "band"), None), P(), P()),
        out_specs=P(None, "band", None, "blk", None),
        check_vma=False,
    )
```

```python
import math

import jax
import jax.numpy as jnp
import numpy as np
from jax import lax
from jax.experimental import pallas as pl
from jax.experimental.pallas import tpu as pltpu
from jax.sharding import PartitionSpec as P

C = 4096
TAPS = 16
NSPEC = 12
FRAMES = NSPEC + TAPS - 1
EL = 16
LANES = 128
BANDS = 8
SLOTS = 8
GROUPS = 4
GROUP_W = C // GROUPS
CHUNK = 512
N_CENTRE = 4
N_CHUNK = C // CHUNK
MESH = pl.DeviceIdType.MESH
F32, BF16 = jnp.float32, jnp.bfloat16


def taper_table():
    idx = np.arange(TAPS * C, dtype=np.float64)
    centre = (idx + 0.5) / C - TAPS / 2.0
    window = 0.5 - 0.5 * np.cos(2.0 * math.pi * (idx + 0.5) / (TAPS * C))
    prototype = np.sinc(centre) * window
    prototype = prototype / np.sqrt(np.sum(prototype * prototype))
    return prototype.reshape(TAPS, C).astype(np.float32)


def cos_sin(turns):
    shifted = turns + 512
    quarter = (shifted >> 10) & 3
    x = ((shifted & 1023) - 512).astype(F32) * (2.0 * math.pi / 4096.0)
    x2 = x * x
    s = x * (1.0 + x2 * (-1.0 / 6 + x2 * (1.0 / 120 + x2 * (-1.0 / 5040 + x2 * (1.0 / 362880)))))
    c = 1.0 + x2 * (-0.5 + x2 * (1.0 / 24 + x2 * (-1.0 / 720 + x2 * (1.0 / 40320))))
    odd = (quarter & 1) == 1
    cc, ss = jnp.where(odd, s, c), jnp.where(odd, c, s)
    cc = jnp.where((quarter == 1) | (quarter == 2), -cc, cc)
    ss = jnp.where(quarter >= 2, -ss, ss)
    return cc, ss


def split(y):
    hi = y.astype(BF16)
    return hi, (y - hi.astype(F32)).astype(BF16)


CENTRE = tuple(range(TAPS // 2 - N_CENTRE // 2, TAPS // 2 + N_CENTRE // 2))
OUTER = tuple(p for p in range(TAPS) if p not in CENTRE)
ROWS = 2 * NSPEC * EL


def front_kernel(
    n_band, n_blk, volt, chans_hbm, taper_hbm, x, chans, taper, small_sems, samples, base_c, base_s,
    step_c, step_s, table, lhs_a, lhs_b, total, sems, z, held, ct_send, ct_recv, ag_send, ag_recv,
    fw_send, fw_recv, here,
):
    greet(n_band, n_blk)
    def fetch(group, frame):
        return pltpu.make_async_copy(
            volt.at[:, :, pl.ds(frame * C + group * GROUP_W, GROUP_W)],
            samples.at[group, frame],
            sems.at[group],
        )

    small = [
        pltpu.make_async_copy(chans_hbm, chans, small_sems.at[0]),
        pltpu.make_async_copy(taper_hbm, taper, small_sems.at[1]),
    ]
    for copy in small:
        copy.start()
    for group in range(GROUPS):
        for frame in range(FRAMES):
            fetch(group, frame).start()
    small[0].wait()

    lane = lax.broadcasted_iota(jnp.int32, (8, LANES), 1)
    key = ((lane >> 4) << 3) + (lane & 7)
    row = jnp.zeros((8, LANES), jnp.int32)
    for g in range(BANDS):
        for s in range(SLOTS):
            row = jnp.where(key == g * SLOTS + s, chans[g, s], row)
    quarter_turn = ((lane[:1] >> 3) & 1) * 1024
    row = row[:1]
    inner = lax.broadcasted_iota(jnp.int32, (LANES, LANES), 0)
    c0, s0 = cos_sin((inner * row + quarter_turn) & 4095)
    base_c[...] = c0
    base_s[...] = s0
    outer = lax.broadcasted_iota(jnp.int32, (C // LANES, LANES), 0) * LANES
    c1, s1 = cos_sin((outer * row) & 4095)
    step_c[...] = c1
    step_s[...] = s1

    def build(chunk, carry):
        for part in range(CHUNK // LANES):
            a = chunk * (CHUNK // LANES) + part
            ca, sa = step_c[pl.ds(a, 1), :], step_s[pl.ds(a, 1), :]
            hi, lo = split(ca * base_c[...] - sa * base_s[...])
            rows = slice(part * LANES, (part + 1) * LANES)
            table[chunk, rows, :LANES] = hi
            table[chunk, rows, LANES:] = lo
        return carry

    lax.fori_loop(0, N_CHUNK, build, 0)

    def weigh(chunk, lhs):
        group = chunk // (GROUP_W // CHUNK)
        for part in range(CHUNK // LANES):
            k = pl.multiple_of(chunk * CHUNK + part * LANES, LANES)
            in_group = pl.multiple_of(k - group * GROUP_W, LANES)
            taps = [
                jnp.broadcast_to(taper[p : p + 1, pl.ds(k, LANES)], (EL, LANES))
                for p in range(TAPS)
            ]
            taps = [taps[p] if p in CENTRE else taps[p].astype(BF16) for p in range(TAPS)]
            column = slice(part * LANES, (part + 1) * LANES)
            for comp in range(2):
                side, mid = [None] * NSPEC, [None] * NSPEC
                for f in range(FRAMES):
                    x = samples[group, f, comp, :, pl.ds(in_group, LANES)]
                    wide = x.astype(F32)
                    for t in range(max(0, f - TAPS + 1), min(NSPEC - 1, f) + 1):
                        p = f - t
                        if p in CENTRE:
                            term = taps[p] * wide
                            mid[t] = term if mid[t] is None else mid[t] + term
                        else:
                            term = taps[p] * x
                            side[t] = term if side[t] is None else side[t] + term
                    if f >= TAPS - 1:
                        t = f - TAPS + 1
                        hi, lo = split(mid[t] + side[t].astype(F32))
                        at = (comp * NSPEC + t) * EL
                        lhs[at : at + EL, column] = hi
                        lhs[ROWS + at : ROWS + at + EL, column] = lo

    def transform(chunk, lhs):
        r = jnp.dot(lhs[...], table[chunk], preferred_element_type=F32)
        total[...] += (r[:ROWS, LANES:] + r[ROWS:, :LANES]) + r[:ROWS, :LANES]

    def wait_group(group):
        pltpu.make_async_copy(samples.at[group], samples.at[group], sems.at[group]).wait()

    small[1].wait()
    total[...] = jnp.zeros_like(total)
    lhs_b[...] = jnp.zeros_like(lhs_b)

    per_group = GROUP_W // CHUNK

    def two_chunks(i, carry):
        first = i * 2
        weigh(first, lhs_a)
        transform(lax.max(first - 1, 0), lhs_b)
        weigh(first + 1, lhs_b)
        transform(first, lhs_a)
        return carry

    for group in range(GROUPS):
        wait_group(group)
        lax.fori_loop(group * per_group // 2, (group + 1) * per_group // 2, two_chunks, 0)
    transform(N_CHUNK - 1, lhs_b)

    is_real = (lax.broadcasted_iota(jnp.int32, (EL, LANES), 1) & 8) == 0
    y = []
    for t in range(NSPEC):
        re = total[t * EL : (t + 1) * EL, :]
        im = total[(NSPEC + t) * EL : (NSPEC + t + 1) * EL, :]
        swapped = jnp.where(is_real, -pltpu.roll(im, LANES - 8, 1), pltpu.roll(im, 8, 1))
        y.append(re + swapped)
    place = lax.broadcasted_iota(jnp.int32, (EL, LANES), 1) >> 4
    for g in range(BANDS):
        for tile in range(2):
            out = jnp.zeros((EL, LANES), F32)
            for t in range(tile * 8, min(tile * 8 + 8, NSPEC)):
                moved = y[t]
                shift = (t - g) * 16 % LANES
                if shift:
                    moved = pltpu.roll(moved, shift, 1)
                out = jnp.where(place == t - tile * 8, moved, out)
            z[g, :, tile * LANES : (tile + 1) * LANES] = out.astype(BF16)
    share(
        n_band, n_blk, z, x, held, ct_send, ct_recv, ag_send, ag_recv, fw_send, fw_recv, here
    )


def places(n_band, n_blk):
    g, b = lax.axis_index("band"), lax.axis_index("blk")
    core, near, along = b % 2, b // 2 % 2, b // 4
    n_along = n_blk // 4

    def chip(d_along, d_near):
        return ((along + d_along + n_along) % n_along * 2 + (near + d_near) % 2) * 2 + core

    return g, b, b + 1 - 2 * core, chip


STEPS = ((1, 0), (-1, 0), (0, 1), (1, 1), (-1, 1))
PASSED = ((0, 0, 0), (1, 1, 1), (3, 0, 0), (4, 1, 1))


def greet(n_band, n_blk):
    g, b, sibling, chip = places(n_band, n_blk)
    peers = [((g + d) % n_band, b) for d in range(1, n_band)]
    peers += [(g, chip(*step)) for step in STEPS] + [(g, sibling)]
    barrier = pltpu.get_barrier_semaphore()
    for peer in peers:
        pl.semaphore_signal(barrier, inc=1, device_id=peer, device_id_type=MESH)


def share(n_band, n_blk, z, x, held, ct_send, ct_recv, ag_send, ag_recv, fw_send, fw_recv, here):
    g, b, sibling, chip = places(n_band, n_blk)
    pl.semaphore_wait(pltpu.get_barrier_semaphore(), n_band - 1 + len(STEPS) + 1)
    block = EL * n_band
    half = block // 2

    def rows(owner, part=None):
        if part is None:
            return pl.ds(pl.multiple_of(owner * block, block), block)
        return pl.ds(pl.multiple_of(owner * block + part * half, half), half)

    def remote(src, dst, send, recv, to):
        copy = pltpu.make_async_remote_copy(src, dst, send, recv, to, MESH)
        copy.start()
        return copy

    mine = pl.ds(pl.multiple_of(b * block + g * EL, EL), EL)
    turns = []
    for d in range(1, n_band):
        to = (g + d) % n_band
        turns.append(remote(z.at[to], held.at[mine], ct_send.at[d], ct_recv.at[d], (to, b)))
    keep = pltpu.make_async_copy(z.at[g], held.at[mine], here.at[0])
    keep.start()
    keep.wait()
    for turn in turns:
        turn.wait()

    me = rows(b)
    sends = [
        remote(held.at[me], held.at[me], ag_send.at[n], ag_recv.at[n], (g, chip(*step)))
        for n, step in enumerate(STEPS)
    ]
    passed, kept = [], []

    def hand_over(at, n):
        passed.append(remote(held.at[at], x.at[at], fw_send.at[n], fw_recv.at[n], (g, sibling)))
        kept.append(pltpu.make_async_copy(held.at[at], x.at[at], here.at[1 + n]))
        kept[-1].start()

    n_steps = len(STEPS)
    hand_over(me, 0)
    onward = [None] * len(PASSED)
    for n, (da, dn) in enumerate(STEPS):
        sends[n].wait_recv()
        owner = chip(-da, dn)
        for m, (brought, taken, part) in enumerate(PASSED):
            if brought == n:
                piece = held.at[rows(owner, part)]
                onward[m] = remote(
                    piece, piece, ag_send.at[n_steps + m], ag_recv.at[n_steps + m],
                    (g, chip(*STEPS[taken])),
                )
        hand_over(rows(owner), 1 + n)
    for m, (brought, taken, part) in enumerate(PASSED):
        onward[m].wait_recv()
        da = STEPS[brought][0] + STEPS[taken][0]
        hand_over(rows(chip(-da, STEPS[brought][1]), part), 1 + n_steps + m)
    for copy in kept:
        copy.wait()
    for copy in sends + onward:
        copy.wait_send()
    for copy in passed:
        copy.wait()


def front(volt, chans, n_band, n_blk):
    hbm = pl.BlockSpec(memory_space=pltpu.HBM)
    dma = pltpu.SemaphoreType.DMA
    everyone = EL * n_band * n_blk
    n_copies = len(STEPS) + len(PASSED)

    def body(*refs):
        front_kernel(n_band, n_blk, *refs)

    return pl.pallas_call(
        body,
        out_shape=jax.ShapeDtypeStruct((everyone, 2 * LANES), BF16),
        in_specs=[hbm] * 3,
        out_specs=hbm,
        scratch_shapes=[
            pltpu.SMEM((BANDS, SLOTS), jnp.int32),
            pltpu.VMEM((TAPS, C), F32),
            dma((2,)),
            pltpu.VMEM((GROUPS, FRAMES, 2, EL, GROUP_W), BF16),
            pltpu.VMEM((LANES, LANES), F32),
            pltpu.VMEM((LANES, LANES), F32),
            pltpu.VMEM((C // LANES, LANES), F32),
            pltpu.VMEM((C // LANES, LANES), F32),
            pltpu.VMEM((N_CHUNK, CHUNK, 2 * LANES), BF16),
            pltpu.VMEM((2 * ROWS, CHUNK), BF16),
            pltpu.VMEM((2 * ROWS, CHUNK), BF16),
            pltpu.VMEM((ROWS, LANES), F32),
            dma((GROUPS,)),
            pltpu.VMEM((BANDS, EL, 2 * LANES), BF16),
            pltpu.VMEM((everyone, 2 * LANES), BF16),
            dma((n_band,)),
            dma((n_band,)),
            dma((n_copies,)),
            dma((n_copies,)),
            dma((n_copies + 1,)),
            dma((n_copies + 1,)),
            dma((n_copies + 2,)),
        ],
        compiler_params=pltpu.CompilerParams(
            vmem_limit_bytes=48 * 2**20, collective_id=0, has_side_effects=True
        ),
        name="spectra",
    )(volt, chans, jnp.asarray(taper_table()))


COLUMNS = 512


def correlate_kernel(x_hbm, count, out, lhs, x, sems):
    j = pl.program_id(0)
    block = out.shape[3]
    b = lax.axis_index("blk")

    def fetch(step):
        at = pl.ds(pl.multiple_of(step * COLUMNS, COLUMNS), COLUMNS)
        return pltpu.make_async_copy(x_hbm.at[at], x.at[at], sems.at[step])

    mine = pl.ds(pl.multiple_of(b * block, block), block)
    own_ref = x.at[pl.ds(x_hbm.shape[0], block)]

    @pl.when(j == 0)
    def _():
        first = pltpu.make_async_copy(x_hbm.at[mine], own_ref, sems.at[pl.num_programs(0)])
        first.start()
        for step in range(x_hbm.shape[0] // COLUMNS):
            fetch(step).start()
        first.wait()
        live = count[lax.axis_index("band")]
        lane = lax.broadcasted_iota(jnp.int32, (block, LANES), 1)
        slot = lane & 7
        is_real = (lane & 8) == 0
        for tile in range(2):
            cols = slice(tile * LANES, (tile + 1) * LANES)
            own = own_ref[:, cols].astype(F32)
            turned = jnp.where(
                is_real, pltpu.roll(own, LANES - 8, 1), -pltpu.roll(own, 8, 1)
            )
            own = jnp.where(slot < live, own, 0.0)
            turned = jnp.where(slot < live, turned, 0.0)
            if tile == 1:
                used = lane < (NSPEC - 8) * 16
                own, turned = jnp.where(used, own, 0.0), jnp.where(used, turned, 0.0)
            for s in range(SLOTS):
                for part, value in ((0, own), (1, turned)):
                    at = (part * SLOTS + s) * block
                    lhs[at : at + block, cols] = jnp.where(slot == s, value, 0.0).astype(BF16)

    fetch(j).wait()
    right = x[pl.ds(pl.multiple_of(j * COLUMNS, COLUMNS), COLUMNS), :]
    y = lax.dot_general(
        lhs[...], right, (((1,), (1,)), ((), ())), preferred_element_type=F32
    )
    y = (y * (1.0 / NSPEC)).astype(BF16)
    for part in range(2):
        for s in range(SLOTS):
            at = (part * SLOTS + s) * block
            out[part, 0, s] = y[at : at + block]


def correlate(x, count, n_band, n_blk):
    everyone = x.shape[0]
    block = everyone // n_blk
    return pl.pallas_call(
        correlate_kernel,
        grid=(everyone // COLUMNS,),
        out_shape=jax.ShapeDtypeStruct((2, 1, SLOTS, block, everyone), BF16),
        in_specs=[
            pl.BlockSpec(memory_space=pltpu.HBM),
            pl.BlockSpec(memory_space=pltpu.SMEM),
        ],
        out_specs=pl.BlockSpec((2, 1, SLOTS, block, COLUMNS), lambda j: (0, 0, 0, 0, j)),
        scratch_shapes=[
            pltpu.VMEM((2 * SLOTS * block, x.shape[1]), BF16),
            pltpu.VMEM((everyone + block, x.shape[1]), BF16),
            pltpu.SemaphoreType.DMA((everyone // COLUMNS + 1,)),
        ],
        compiler_params=pltpu.CompilerParams(vmem_limit_bytes=32 * 2**20),
        name="correlate",
    )(x, count)


def solution(mesh):
    n_band, n_blk = mesh.shape["band"], mesh.shape["blk"]

    def local(volt, band_chans, band_count):
        x = front(volt, band_chans, n_band, n_blk)
        return correlate(x, band_count, n_band, n_blk)

    return jax.shard_map(
        local,
        mesh=mesh,
        in_specs=(P(None, ("blk", "band"), None), P(), P()),
        out_specs=P(None, "band", None, "blk", None),
        check_vma=False,
    )
```

```python
import math

import jax
import jax.numpy as jnp
import numpy as np
from jax import lax
from jax.experimental import pallas as pl
from jax.experimental.pallas import tpu as pltpu
from jax.sharding import PartitionSpec as P

C = 4096
TAPS = 16
NSPEC = 12
FRAMES = NSPEC + TAPS - 1
EL = 16
LANES = 128
BANDS = 8
SLOTS = 8
GROUPS = 4
GROUP_W = C // GROUPS
CHUNK = 512
N_CENTRE = 4
N_CHUNK = C // CHUNK
MESH = pl.DeviceIdType.MESH
F32, BF16 = jnp.float32, jnp.bfloat16


def taper_table():
    idx = np.arange(TAPS * C, dtype=np.float64)
    centre = (idx + 0.5) / C - TAPS / 2.0
    window = 0.5 - 0.5 * np.cos(2.0 * math.pi * (idx + 0.5) / (TAPS * C))
    prototype = np.sinc(centre) * window
    prototype = prototype / np.sqrt(np.sum(prototype * prototype))
    return prototype.reshape(TAPS, C).astype(np.float32)


def cos_sin(turns):
    shifted = turns + 512
    quarter = (shifted >> 10) & 3
    x = ((shifted & 1023) - 512).astype(F32) * (2.0 * math.pi / 4096.0)
    x2 = x * x
    s = x * (1.0 + x2 * (-1.0 / 6 + x2 * (1.0 / 120 + x2 * (-1.0 / 5040 + x2 * (1.0 / 362880)))))
    c = 1.0 + x2 * (-0.5 + x2 * (1.0 / 24 + x2 * (-1.0 / 720 + x2 * (1.0 / 40320))))
    odd = (quarter & 1) == 1
    cc, ss = jnp.where(odd, s, c), jnp.where(odd, c, s)
    cc = jnp.where((quarter == 1) | (quarter == 2), -cc, cc)
    ss = jnp.where(quarter >= 2, -ss, ss)
    return cc, ss


def split(y):
    hi = y.astype(BF16)
    return hi, (y - hi.astype(F32)).astype(BF16)


CENTRE = tuple(range(TAPS // 2 - N_CENTRE // 2, TAPS // 2 + N_CENTRE // 2))
OUTER = tuple(p for p in range(TAPS) if p not in CENTRE)
EARLY, LATE = range(8), range(8, NSPEC)


def front_kernel(
    n_band, n_blk, volt, chans_hbm, taper_hbm, x0, x1, chans, taper, small_sems, samples, base_c,
    base_s, step_c, step_s, table, lhs_a, lhs_b, total, sems, z0, z1, turned, held0, held1, *comm_sems
):
    greet(n_band, n_blk)
    def fetch(group, frame):
        return pltpu.make_async_copy(
            volt.at[:, :, pl.ds(frame * C + group * GROUP_W, GROUP_W)],
            samples.at[group, frame],
            sems.at[group],
        )

    small = [
        pltpu.make_async_copy(chans_hbm, chans, small_sems.at[0]),
        pltpu.make_async_copy(taper_hbm, taper, small_sems.at[1]),
    ]
    for copy in small:
        copy.start()
    for group in range(GROUPS):
        for frame in range(FRAMES):
            fetch(group, frame).start()
    small[0].wait()

    lane = lax.broadcasted_iota(jnp.int32, (8, LANES), 1)
    key = ((lane >> 4) << 3) + (lane & 7)
    row = jnp.zeros((8, LANES), jnp.int32)
    for g in range(BANDS):
        for s in range(SLOTS):
            row = jnp.where(key == g * SLOTS + s, chans[g, s], row)
    quarter_turn = ((lane[:1] >> 3) & 1) * 1024
    row = row[:1]
    inner = lax.broadcasted_iota(jnp.int32, (LANES, LANES), 0)
    c0, s0 = cos_sin((inner * row + quarter_turn) & 4095)
    base_c[...] = c0
    base_s[...] = s0
    outer = lax.broadcasted_iota(jnp.int32, (C // LANES, LANES), 0) * LANES
    c1, s1 = cos_sin((outer * row) & 4095)
    step_c[...] = c1
    step_s[...] = s1

    def build(chunk, carry):
        for part in range(CHUNK // LANES):
            a = chunk * (CHUNK // LANES) + part
            ca, sa = step_c[pl.ds(a, 1), :], step_s[pl.ds(a, 1), :]
            hi, lo = split(ca * base_c[...] - sa * base_s[...])
            rows = slice(part * LANES, (part + 1) * LANES)
            table[chunk, rows, :LANES] = hi
            table[chunk, rows, LANES:] = lo
        return carry

    lax.fori_loop(0, N_CHUNK, build, 0)

    def weigh(chunk, lhs, ts):
        rows = 2 * len(ts) * EL
        group = chunk // (GROUP_W // CHUNK)
        for part in range(CHUNK // LANES):
            k = pl.multiple_of(chunk * CHUNK + part * LANES, LANES)
            in_group = pl.multiple_of(k - group * GROUP_W, LANES)
            taps = [
                jnp.broadcast_to(taper[p : p + 1, pl.ds(k, LANES)], (EL, LANES))
                for p in range(TAPS)
            ]
            taps = [taps[p] if p in CENTRE else taps[p].astype(BF16) for p in range(TAPS)]
            column = slice(part * LANES, (part + 1) * LANES)
            for comp in range(2):
                side, mid = [None] * NSPEC, [None] * NSPEC
                for f in range(ts[0], ts[-1] + TAPS):
                    x = samples[group, f, comp, :, pl.ds(in_group, LANES)]
                    wide = x.astype(F32)
                    for t in range(max(ts[0], f - TAPS + 1), min(ts[-1], f) + 1):
                        p = f - t
                        if p in CENTRE:
                            term = taps[p] * wide
                            mid[t] = term if mid[t] is None else mid[t] + term
                        else:
                            term = taps[p] * x
                            side[t] = term if side[t] is None else side[t] + term
                    if f >= ts[0] + TAPS - 1:
                        t = f - TAPS + 1
                        hi, lo = split(mid[t] + side[t].astype(F32))
                        at = (comp * len(ts) + t - ts[0]) * EL
                        lhs[at : at + EL, column] = hi
                        lhs[rows + at : rows + at + EL, column] = lo

    def transform(chunk, lhs, ts):
        rows = 2 * len(ts) * EL
        at = 2 * ts[0] * EL
        r = jnp.dot(lhs[: 2 * rows, :], table[chunk], preferred_element_type=F32)
        total[at : at + rows, :] += (r[:rows, LANES:] + r[rows:, :LANES]) + r[:rows, :LANES]

    def wait_group(group):
        pltpu.make_async_copy(samples.at[group], samples.at[group], sems.at[group]).wait()

    small[1].wait()
    total[...] = jnp.zeros_like(total)
    per_group = GROUP_W // CHUNK

    def spectra_of(ts, first_pass):
        lhs_b[...] = jnp.zeros_like(lhs_b)

        def two_chunks(i, carry):
            first = i * 2
            weigh(first, lhs_a, ts)
            transform(lax.max(first - 1, 0), lhs_b, ts)
            weigh(first + 1, lhs_b, ts)
            transform(first, lhs_a, ts)
            return carry

        if first_pass:
            for group in range(GROUPS):
                wait_group(group)
                lax.fori_loop(
                    group * per_group // 2, (group + 1) * per_group // 2, two_chunks, 0
                )
        else:
            lax.fori_loop(0, N_CHUNK // 2, two_chunks, 0)
        transform(N_CHUNK - 1, lhs_b, ts)

    is_real = (lax.broadcasted_iota(jnp.int32, (EL, LANES), 1) & 8) == 0
    place = lax.broadcasted_iota(jnp.int32, (EL, LANES), 1) >> 4

    def by_band(ts, z):
        y = []
        for n in range(len(ts)):
            at = (2 * ts[0] + n) * EL
            re = total[at : at + EL, :]
            im = total[at + len(ts) * EL : at + (len(ts) + 1) * EL, :]
            swapped = jnp.where(is_real, -pltpu.roll(im, LANES - 8, 1), pltpu.roll(im, 8, 1))
            y.append(re + swapped)
        for g in range(BANDS):
            out = jnp.zeros((EL, LANES), F32)
            for n in range(len(ts)):
                shift = (n - g) * 16 % LANES
                moved = pltpu.roll(y[n], shift, 1) if shift else y[n]
                out = jnp.where(place == n, moved, out)
            z[g] = out.astype(BF16)

    early, late = Exchange(n_band, n_blk, 0, comm_sems), Exchange(n_band, n_blk, 1, comm_sems)
    spectra_of(EARLY, True)
    by_band(EARLY, z0)
    pl.semaphore_wait(pltpu.get_barrier_semaphore(), n_band - 1 + len(STEPS) + 1)
    block = EL * n_band
    mine = pl.ds(pl.multiple_of(lax.axis_index("blk") * block, block), block)
    early.turn(z0, held0.at[mine])
    spectra_of(LATE, False)
    by_band(LATE, z1)
    late.turn(z1, turned)
    early.turn_done()
    early.spread(held0, x0, block)
    early.pass_on()
    late.turn_done()
    half = block // 2
    top, bottom = turned[:half].astype(F32), turned[half:].astype(F32)
    packed = jnp.where(place[:1] < len(LATE), top, pltpu.roll(bottom, LANES // 2, 1)).astype(BF16)
    held1[pl.ds(pl.multiple_of(lax.axis_index("blk") * half, half), half), :] = packed
    late.spread(held1, x1, half)
    early.arrive()
    late.pass_on()
    late.arrive()
    early.finish()
    late.finish()


def places(n_band, n_blk):
    g, b = lax.axis_index("band"), lax.axis_index("blk")
    core, near, along = b % 2, b // 2 % 2, b // 4
    n_along = n_blk // 4

    def chip(d_along, d_near):
        return ((along + d_along + n_along) % n_along * 2 + (near + d_near) % 2) * 2 + core

    return g, b, b + 1 - 2 * core, chip


STEPS = ((1, 0), (-1, 0), (0, 1), (1, 1), (-1, 1))
PASSED = ((0, 0, 0), (1, 1, 1), (3, 0, 0), (4, 1, 1))


def greet(n_band, n_blk):
    g, b, sibling, chip = places(n_band, n_blk)
    peers = [((g + d) % n_band, b) for d in range(1, n_band)]
    peers += [(g, chip(*step)) for step in STEPS] + [(g, sibling)]
    barrier = pltpu.get_barrier_semaphore()
    for peer in peers:
        pl.semaphore_signal(barrier, inc=1, device_id=peer, device_id_type=MESH)


class Exchange:
    def __init__(self, n_band, n_blk, tile, sems):
        self.n_band = n_band
        self.g, self.b, self.sibling, self.chip = places(n_band, n_blk)
        self.sems = [sem.at[tile] for sem in sems]
        self.sends, self.onward, self.passed, self.kept = [], [], [], []

    def remote(self, src, dst, send, recv, to):
        copy = pltpu.make_async_remote_copy(src, dst, send, recv, to, MESH)
        copy.start()
        return copy

    def turn(self, z, block):
        g, send, recv, here = self.g, self.sems[0], self.sems[1], self.sems[6]
        mine = pl.ds(pl.multiple_of(g * EL, EL), EL)
        self.turns = []
        for d in range(1, self.n_band):
            to = (g + d) % self.n_band
            self.turns.append(
                self.remote(z.at[to], block.at[mine], send.at[d], recv.at[d], (to, self.b))
            )
        self.turns.append(pltpu.make_async_copy(z.at[g], block.at[mine], here.at[0]))
        self.turns[-1].start()

    def turn_done(self):
        for turn in self.turns:
            turn.wait()

    def rows(self, owner, part=None):
        if part is None:
            return pl.ds(pl.multiple_of(owner * self.block, self.block), self.block)
        half = self.block // 2
        return pl.ds(pl.multiple_of(owner * self.block + part * half, half), half)

    def hand_over(self, at, n):
        held, x, here = self.held, self.x, self.sems[6]
        self.passed.append(
            self.remote(
                held.at[at], x.at[at], self.sems[4].at[n], self.sems[5].at[n], (self.g, self.sibling)
            )
        )
        self.kept.append(pltpu.make_async_copy(held.at[at], x.at[at], here.at[1 + n]))
        self.kept[-1].start()

    def spread(self, held, x, block):
        self.held, self.x, self.block = held, x, block
        me = held.at[self.rows(self.b)]
        for n, step in enumerate(STEPS):
            self.sends.append(
                self.remote(
                    me, me, self.sems[2].at[n], self.sems[3].at[n], (self.g, self.chip(*step))
                )
            )
        self.hand_over(self.rows(self.b), 0)

    def pass_on(self):
        self.onward = [None] * len(PASSED)
        for n, (da, dn) in enumerate(STEPS):
            self.sends[n].wait_recv()
            owner = self.chip(-da, dn)
            for m, (brought, taken, part) in enumerate(PASSED):
                if brought == n:
                    piece = self.held.at[self.rows(owner, part)]
                    at = len(STEPS) + m
                    to = (self.g, self.chip(*STEPS[taken]))
                    self.onward[m] = self.remote(
                        piece, piece, self.sems[2].at[at], self.sems[3].at[at], to
                    )
            self.hand_over(self.rows(owner), 1 + n)

    def arrive(self):
        for m, (brought, taken, part) in enumerate(PASSED):
            self.onward[m].wait_recv()
            da = STEPS[brought][0] + STEPS[taken][0]
            owner = self.chip(-da, STEPS[brought][1])
            self.hand_over(self.rows(owner, part), 1 + len(STEPS) + m)

    def finish(self):
        for copy in self.kept:
            copy.wait()
        for copy in self.sends + self.onward:
            copy.wait_send()
        for copy in self.passed:
            copy.wait()


def front(volt, chans, n_band, n_blk):
    hbm = pl.BlockSpec(memory_space=pltpu.HBM)
    dma = pltpu.SemaphoreType.DMA
    everyone = EL * n_band * n_blk
    n_copies = len(STEPS) + len(PASSED)

    def body(*refs):
        front_kernel(n_band, n_blk, *refs)

    return pl.pallas_call(
        body,
        out_shape=[
            jax.ShapeDtypeStruct((everyone, LANES), BF16),
            jax.ShapeDtypeStruct((everyone // 2, LANES), BF16),
        ],
        in_specs=[hbm] * 3,
        out_specs=[hbm] * 2,
        scratch_shapes=[
            pltpu.SMEM((BANDS, SLOTS), jnp.int32),
            pltpu.VMEM((TAPS, C), F32),
            dma((2,)),
            pltpu.VMEM((GROUPS, FRAMES, 2, EL, GROUP_W), BF16),
            pltpu.VMEM((LANES, LANES), F32),
            pltpu.VMEM((LANES, LANES), F32),
            pltpu.VMEM((C // LANES, LANES), F32),
            pltpu.VMEM((C // LANES, LANES), F32),
            pltpu.VMEM((N_CHUNK, CHUNK, 2 * LANES), BF16),
            pltpu.VMEM((4 * len(EARLY) * EL, CHUNK), BF16),
            pltpu.VMEM((4 * len(EARLY) * EL, CHUNK), BF16),
            pltpu.VMEM((2 * NSPEC * EL, LANES), F32),
            dma((GROUPS,)),
            pltpu.VMEM((BANDS, EL, LANES), BF16),
            pltpu.VMEM((BANDS, EL, LANES), BF16),
            pltpu.VMEM((EL * n_band, LANES), BF16),
            pltpu.VMEM((everyone, LANES), BF16),
            pltpu.VMEM((everyone // 2, LANES), BF16),
            dma((2, n_band)),
            dma((2, n_band)),
            dma((2, n_copies)),
            dma((2, n_copies)),
            dma((2, n_copies + 1)),
            dma((2, n_copies + 1)),
            dma((2, n_copies + 2)),
        ],
        compiler_params=pltpu.CompilerParams(
            vmem_limit_bytes=60 * 2**20, collective_id=0, has_side_effects=True
        ),
        name="spectra",
    )(volt, chans, jnp.asarray(taper_table()))


COLUMNS = 512


def correlate_kernel(x0_hbm, x1_hbm, count, out, lhs, right, x0, x1, sems):
    j = pl.program_id(0)
    steps = x0_hbm.shape[0] // COLUMNS
    block = out.shape[3]
    half = block // 2
    b = lax.axis_index("blk")
    low = lax.broadcasted_iota(jnp.int32, (half, LANES), 1) < LANES // 2

    def fetch(step):
        pairs = []
        for n, (hbm, x) in enumerate(((x0_hbm, x0), (x1_hbm, x1))):
            width = COLUMNS // (1 + n)
            at = pl.ds(pl.multiple_of(step * width, width), width)
            pairs.append(pltpu.make_async_copy(hbm.at[at], x.at[at], sems.at[n, step]))
        return pairs

    def whole(packed):
        packed = packed.astype(F32)
        return packed, pltpu.roll(packed, LANES // 2, 1)

    @pl.when(j == 0)
    def _():
        own = []
        for n, (hbm, x) in enumerate(((x0_hbm, x0), (x1_hbm, x1))):
            rows = block // (1 + n)
            to = x.at[pl.ds(hbm.shape[0], rows)]
            at = pl.ds(pl.multiple_of(b * rows, rows), rows)
            own.append(pltpu.make_async_copy(hbm.at[at], to, sems.at[n, steps]))
            own[-1].start()
        for step in range(steps):
            for copy in fetch(step):
                copy.start()
        for copy in own:
            copy.wait()
        live = count[lax.axis_index("band")]

        def fill(own, at, cols, used):
            lane = lax.broadcasted_iota(jnp.int32, own.shape, 1)
            slot = lane & 7
            turned = jnp.where(
                (lane & 8) == 0, pltpu.roll(own, LANES - 8, 1), -pltpu.roll(own, 8, 1)
            )
            keep = (slot < live) & (lane < used)
            own, turned = jnp.where(keep, own, 0.0), jnp.where(keep, turned, 0.0)
            for s in range(SLOTS):
                for part, value in ((0, own), (1, turned)):
                    to = (part * SLOTS + s) * block + at
                    lhs[to : to + own.shape[0], cols] = jnp.where(slot == s, value, 0.0).astype(BF16)

        fill(x0[pl.ds(x0_hbm.shape[0], block), :].astype(F32), 0, slice(0, LANES), LANES)
        for n, part in enumerate(whole(x1[pl.ds(x1_hbm.shape[0], half), :])):
            fill(part, n * half, slice(LANES, 2 * LANES), len(LATE) * 16)

    for copy in fetch(j):
        copy.wait()
    right[:, :LANES] = x0[pl.ds(pl.multiple_of(j * COLUMNS, COLUMNS), COLUMNS), :]
    for n in range(COLUMNS // block):
        at = pl.multiple_of(j * (COLUMNS // 2) + n * half, half)
        first, second = whole(x1[pl.ds(at, half), :])
        for m, part in enumerate((first, second)):
            part = jnp.where(low, part, 0.0).astype(BF16)
            right[n * block + m * half : n * block + (m + 1) * half, LANES:] = part
    y = lax.dot_general(
        lhs[...], right[...], (((1,), (1,)), ((), ())), preferred_element_type=F32
    )
    y = (y * (1.0 / NSPEC)).astype(BF16)
    for part in range(2):
        for s in range(SLOTS):
            at = (part * SLOTS + s) * block
            out[part, 0, s] = y[at : at + block]


def correlate(x0, x1, count, n_band, n_blk):
    everyone = x0.shape[0]
    block = everyone // n_blk
    hbm = pl.BlockSpec(memory_space=pltpu.HBM)
    return pl.pallas_call(
        correlate_kernel,
        grid=(everyone // COLUMNS,),
        out_shape=jax.ShapeDtypeStruct((2, 1, SLOTS, block, everyone), BF16),
        in_specs=[hbm, hbm, pl.BlockSpec(memory_space=pltpu.SMEM)],
        out_specs=pl.BlockSpec((2, 1, SLOTS, block, COLUMNS), lambda j: (0, 0, 0, 0, j)),
        scratch_shapes=[
            pltpu.VMEM((2 * SLOTS * block, 2 * LANES), BF16),
            pltpu.VMEM((COLUMNS, 2 * LANES), BF16),
            pltpu.VMEM((everyone + block, LANES), BF16),
            pltpu.VMEM(((everyone + block) // 2, LANES), BF16),
            pltpu.SemaphoreType.DMA((2, everyone // COLUMNS + 1)),
        ],
        compiler_params=pltpu.CompilerParams(vmem_limit_bytes=60 * 2**20),
        name="correlate",
    )(x0, x1, count)


def solution(mesh):
    n_band, n_blk = mesh.shape["band"], mesh.shape["blk"]

    def local(volt, band_chans, band_count):
        x0, x1 = front(volt, band_chans, n_band, n_blk)
        return correlate(x0, x1, band_count, n_band, n_blk)

    return jax.shard_map(
        local,
        mesh=mesh,
        in_specs=(P(None, ("blk", "band"), None), P(), P()),
        out_specs=P(None, "band", None, "blk", None),
        check_vma=False,
    )
```

```python
import math

import jax
import jax.numpy as jnp
import numpy as np
from jax import lax
from jax.experimental import pallas as pl
from jax.experimental.pallas import tpu as pltpu
from jax.sharding import PartitionSpec as P

C = 4096
TAPS = 16
NSPEC = 12
FRAMES = NSPEC + TAPS - 1
EL = 16
LANES = 128
BANDS = 8
SLOTS = 8
GROUPS = 4
GROUP_W = C // GROUPS
CHUNK = 512
N_CENTRE = 4
N_CHUNK = C // CHUNK
MESH = pl.DeviceIdType.MESH
F32, BF16 = jnp.float32, jnp.bfloat16


def taper_scale():
    idx = np.arange(TAPS * C, dtype=np.float64)
    centre = (idx + 0.5) / C - TAPS / 2.0
    window = 0.5 - 0.5 * np.cos(2.0 * math.pi * (idx + 0.5) / (TAPS * C))
    prototype = np.sinc(centre) * window
    return float(1.0 / np.sqrt(np.sum(prototype * prototype)))


def half_sine(x):
    y = jnp.minimum(x, math.pi - x)
    y2 = y * y
    s = 1.0 / 120 + y2 * (-1.0 / 5040 + y2 * (1.0 / 362880 + y2 * (-1.0 / 39916800)))
    return y * (1.0 + y2 * (-1.0 / 6 + y2 * s))


def fill_taper(taper):
    width = 512
    scale = taper_scale() / math.pi

    def some(n, carry):
        tap = lax.broadcasted_iota(jnp.int32, (TAPS, width), 0)
        k = lax.broadcasted_iota(jnp.int32, (TAPS, width), 1) + n * width
        frac = (k.astype(F32) + 0.5) * (1.0 / C)
        top = half_sine(frac * math.pi) * jnp.where((tap & 1) == 0, scale, -scale)
        window = half_sine((tap.astype(F32) + frac) * (math.pi / TAPS))
        value = top * window * window / (frac + (tap - TAPS // 2).astype(F32))
        taper[:, pl.ds(pl.multiple_of(n * width, width), width)] = value
        return carry

    lax.fori_loop(0, C // width, some, 0)


def cos_sin(turns):
    shifted = turns + 512
    quarter = (shifted >> 10) & 3
    x = ((shifted & 1023) - 512).astype(F32) * (2.0 * math.pi / 4096.0)
    x2 = x * x
    s = x * (1.0 + x2 * (-1.0 / 6 + x2 * (1.0 / 120 + x2 * (-1.0 / 5040 + x2 * (1.0 / 362880)))))
    c = 1.0 + x2 * (-0.5 + x2 * (1.0 / 24 + x2 * (-1.0 / 720 + x2 * (1.0 / 40320))))
    odd = (quarter & 1) == 1
    cc, ss = jnp.where(odd, s, c), jnp.where(odd, c, s)
    cc = jnp.where((quarter == 1) | (quarter == 2), -cc, cc)
    ss = jnp.where(quarter >= 2, -ss, ss)
    return cc, ss


def split(y):
    hi = y.astype(BF16)
    return hi, (y - hi.astype(F32)).astype(BF16)


CENTRE = tuple(range(TAPS // 2 - N_CENTRE // 2, TAPS // 2 + N_CENTRE // 2))
OUTER = tuple(p for p in range(TAPS) if p not in CENTRE)
ROWS = 2 * NSPEC * EL


def front_kernel(
    n_band, n_blk, volt, chans_hbm, x, chans, taper, small_sem, samples, base_c, base_s, step_c, step_s,
    table, lhs_a, lhs_b, total, sems, z, turned, ct_send, ct_recv, ag_send, ag_recv, fw_send, fw_recv,
    here,
):
    def fetch(group, frame):
        return pltpu.make_async_copy(
            volt.at[:, :, pl.ds(frame * C + group * GROUP_W, GROUP_W)],
            samples.at[group, frame],
            sems.at[group],
        )

    def fetch_group(group):
        for frame in range(FRAMES):
            fetch(group, frame).start()

    small = pltpu.make_async_copy(chans_hbm, chans, small_sem.at[0])
    small.start()
    fetch_group(0)
    greet(n_band, n_blk)
    fetch_group(1)
    fill_taper(taper)
    small.wait()

    lane = lax.broadcasted_iota(jnp.int32, (8, LANES), 1)
    key = ((lane >> 4) << 3) + (lane & 7)
    row = jnp.zeros((8, LANES), jnp.int32)
    for g in range(BANDS):
        for s in range(SLOTS):
            row = jnp.where(key == g * SLOTS + s, chans[g, s], row)
    quarter_turn = ((lane[:1] >> 3) & 1) * 1024
    row = row[:1]
    inner = lax.broadcasted_iota(jnp.int32, (LANES, LANES), 0)
    c0, s0 = cos_sin((inner * row + quarter_turn) & 4095)
    base_c[...] = c0
    base_s[...] = s0
    outer = lax.broadcasted_iota(jnp.int32, (C // LANES, LANES), 0) * LANES
    c1, s1 = cos_sin((outer * row) & 4095)
    step_c[...] = c1
    step_s[...] = s1

    def build(chunk, carry):
        for part in range(CHUNK // LANES):
            a = chunk * (CHUNK // LANES) + part
            ca, sa = step_c[pl.ds(a, 1), :], step_s[pl.ds(a, 1), :]
            hi, lo = split(ca * base_c[...] - sa * base_s[...])
            rows = slice(part * LANES, (part + 1) * LANES)
            table[chunk, rows, :LANES] = hi
            table[chunk, rows, LANES:] = lo
        return carry

    lax.fori_loop(0, N_CHUNK, build, 0)

    def weigh(chunk, lhs):
        group = chunk // (GROUP_W // CHUNK)
        for part in range(CHUNK // LANES):
            k = pl.multiple_of(chunk * CHUNK + part * LANES, LANES)
            in_group = pl.multiple_of(k - group * GROUP_W, LANES)
            taps = [
                jnp.broadcast_to(taper[p : p + 1, pl.ds(k, LANES)], (EL, LANES))
                for p in range(TAPS)
            ]
            taps = [taps[p] if p in CENTRE else taps[p].astype(BF16) for p in range(TAPS)]
            column = slice(part * LANES, (part + 1) * LANES)
            for comp in range(2):
                side, mid = [None] * NSPEC, [None] * NSPEC
                for f in range(FRAMES):
                    x = samples[group, f, comp, :, pl.ds(in_group, LANES)]
                    wide = x.astype(F32)
                    for t in range(max(0, f - TAPS + 1), min(NSPEC - 1, f) + 1):
                        p = f - t
                        if p in CENTRE:
                            term = taps[p] * wide
                            mid[t] = term if mid[t] is None else mid[t] + term
                        else:
                            term = taps[p] * x
                            side[t] = term if side[t] is None else side[t] + term
                    if f >= TAPS - 1:
                        t = f - TAPS + 1
                        hi, lo = split(mid[t] + side[t].astype(F32))
                        at = (comp * NSPEC + t) * EL
                        lhs[at : at + EL, column] = hi
                        lhs[ROWS + at : ROWS + at + EL, column] = lo

    def transform(chunk, lhs):
        r = jnp.dot(lhs[...], table[chunk], preferred_element_type=F32)
        total[...] += (r[:ROWS, LANES:] + r[ROWS:, :LANES]) + r[:ROWS, :LANES]

    def wait_group(group):
        pltpu.make_async_copy(samples.at[group], samples.at[group], sems.at[group]).wait()

    total[...] = jnp.zeros_like(total)
    lhs_b[...] = jnp.zeros_like(lhs_b)

    per_group = GROUP_W // CHUNK

    def two_chunks(i, carry):
        first = i * 2
        weigh(first, lhs_a)
        transform(lax.max(first - 1, 0), lhs_b)
        weigh(first + 1, lhs_b)
        transform(first, lhs_a)
        return carry

    for group in range(GROUPS):
        if group + 2 < GROUPS:
            fetch_group(group + 2)
        wait_group(group)
        lax.fori_loop(group * per_group // 2, (group + 1) * per_group // 2, two_chunks, 0)
    transform(N_CHUNK - 1, lhs_b)

    is_real = (lax.broadcasted_iota(jnp.int32, (EL, LANES), 1) & 8) == 0
    y = []
    for t in range(NSPEC):
        re = total[t * EL : (t + 1) * EL, :]
        im = total[(NSPEC + t) * EL : (NSPEC + t + 1) * EL, :]
        swapped = jnp.where(is_real, -pltpu.roll(im, LANES - 8, 1), pltpu.roll(im, 8, 1))
        y.append(re + swapped)
    place = lax.broadcasted_iota(jnp.int32, (EL, LANES), 1) >> 4
    for g in range(BANDS):
        for tile in range(2):
            out = jnp.zeros((EL, LANES), F32)
            for t in range(tile * 8, min(tile * 8 + 8, NSPEC)):
                moved = y[t]
                shift = (t - g) * 16 % LANES
                if shift:
                    moved = pltpu.roll(moved, shift, 1)
                out = jnp.where(place == t - tile * 8, moved, out)
            z[g, :, tile * LANES : (tile + 1) * LANES] = out.astype(BF16)
    share(
        n_band, n_blk, z, turned, x, ct_send, ct_recv, ag_send, ag_recv, fw_send, fw_recv, here
    )


def places(n_band, n_blk):
    g, b = lax.axis_index("band"), lax.axis_index("blk")
    core, near, along = b % 2, b // 2 % 2, b // 4
    n_along = n_blk // 4

    def chip(d_along, d_near):
        return ((along + d_along + n_along) % n_along * 2 + (near + d_near) % 2) * 2 + core

    return g, b, b + 1 - 2 * core, chip


STEPS = ((1, 0), (-1, 1), (-1, 0), (1, 1), (0, 1))
PASSED = (0, 1)


def slot_of(d_along, d_near):
    return {0: 0, 1: 2, 3: 4, 2: 6}[d_along % 4] + d_near


PACKED = 192


def greet(n_band, n_blk):
    g, b, sibling, chip = places(n_band, n_blk)
    peers = [((g + d) % n_band, b) for d in range(1, n_band)]
    peers += [(g, chip(*step)) for step in STEPS] + [(g, sibling)]
    barrier = pltpu.get_barrier_semaphore()
    for peer in peers:
        pl.semaphore_signal(barrier, inc=1, device_id=peer, device_id_type=MESH)


def share(n_band, n_blk, z, turned, x, ct_send, ct_recv, ag_send, ag_recv, fw_send, fw_recv, here):
    g, b, sibling, chip = places(n_band, n_blk)
    pl.semaphore_wait(pltpu.get_barrier_semaphore(), n_band - 1 + len(STEPS) + 1)
    half = EL * n_band // 2
    first = b % 2 * (n_blk // 2)

    def slots(start, count=1):
        at = pl.multiple_of((first + start) * PACKED, PACKED)
        return x.at[pl.ds(at, count * PACKED)]

    def remote(src, dst, send, recv, to):
        copy = pltpu.make_async_remote_copy(src, dst, send, recv, to, MESH)
        copy.start()
        return copy

    mine = turned.at[pl.ds(pl.multiple_of(g * EL, EL), EL)]
    turns = []
    for d in range(1, n_band):
        to = (g + d) % n_band
        turns.append(remote(z.at[to], mine, ct_send.at[d], ct_recv.at[d], (to, b)))
    turns.append(pltpu.make_async_copy(z.at[g], mine, here.at[0]))
    turns[-1].start()
    for turn in turns:
        turn.wait()
    own = slots(0)
    low = lax.broadcasted_iota(jnp.int32, (half, LANES), 1) < LANES // 2
    top = turned[:half, LANES:].astype(F32)
    bottom = pltpu.roll(turned[half:, LANES:].astype(F32), LANES // 2, 1)
    own[: 2 * half, :] = turned[:, :LANES]
    own[2 * half :, :] = jnp.where(low, top, bottom).astype(BF16)

    sends = [
        remote(own, slots(slot_of(-da, dn)), ag_send.at[n], ag_recv.at[n], (g, chip(da, dn)))
        for n, (da, dn) in enumerate(STEPS)
    ]
    onward = []
    for n, (da, dn) in enumerate(STEPS):
        sends[n].wait_recv()
        if n in PASSED:
            m = len(STEPS) + len(onward)
            came, goes = slots(slot_of(-da, dn)), slots(slot_of(-2 * da, dn))
            onward.append(remote(came, goes, ag_send.at[m], ag_recv.at[m], (g, chip(da, 0))))
    near = slots(0, len(STEPS) + 1)
    passed = [remote(near, near, fw_send.at[0], fw_recv.at[0], (g, sibling))]
    for copy in onward:
        copy.wait_recv()
    far = slots(len(STEPS) + 1, 2)
    passed.append(remote(far, far, fw_send.at[1], fw_recv.at[1], (g, sibling)))
    for copy in sends + onward:
        copy.wait_send()
    for copy in passed:
        copy.wait()


def front(volt, chans, n_band, n_blk):
    hbm = pl.BlockSpec(memory_space=pltpu.HBM)
    dma = pltpu.SemaphoreType.DMA
    n_copies = len(STEPS) + len(PASSED)
    vmem = pl.BlockSpec(memory_space=pltpu.VMEM)

    def body(*refs):
        front_kernel(n_band, n_blk, *refs)

    return pl.pallas_call(
        body,
        out_shape=jax.ShapeDtypeStruct((n_blk * PACKED, LANES), BF16),
        in_specs=[hbm] * 2,
        out_specs=vmem,
        scratch_shapes=[
            pltpu.SMEM((BANDS, SLOTS), jnp.int32),
            pltpu.VMEM((TAPS, C), F32),
            dma((1,)),
            pltpu.VMEM((GROUPS, FRAMES, 2, EL, GROUP_W), BF16),
            pltpu.VMEM((LANES, LANES), F32),
            pltpu.VMEM((LANES, LANES), F32),
            pltpu.VMEM((C // LANES, LANES), F32),
            pltpu.VMEM((C // LANES, LANES), F32),
            pltpu.VMEM((N_CHUNK, CHUNK, 2 * LANES), BF16),
            pltpu.VMEM((2 * ROWS, CHUNK), BF16),
            pltpu.VMEM((2 * ROWS, CHUNK), BF16),
            pltpu.VMEM((ROWS, LANES), F32),
            dma((GROUPS,)),
            pltpu.VMEM((BANDS, EL, 2 * LANES), BF16),
            pltpu.VMEM((EL * n_band, 2 * LANES), BF16),
            dma((n_band,)),
            dma((n_band,)),
            dma((n_copies,)),
            dma((n_copies,)),
            dma((2,)),
            dma((2,)),
            dma((1,)),
        ],
        compiler_params=pltpu.CompilerParams(
            vmem_limit_bytes=48 * 2**20, collective_id=0, has_side_effects=True
        ),
        name="spectra",
    )(volt, chans)


COLUMNS = 512


def correlate_kernel(n_blk, x, count, out, lhs, right):
    j = pl.program_id(0)
    block = out.shape[3]
    half = block // 2
    b = lax.axis_index("blk")
    near, along = b // 2 % 2, b // 4

    def rows_of(owner):
        d_near = (owner // 2 + near) % 2
        d_along = (owner // 4 - along + n_blk // 4) % (n_blk // 4)
        slot = jnp.where(d_along == 3, 4, jnp.where(d_along == 2, 6, 2 * d_along)) + d_near
        return pl.multiple_of((owner % 2 * (n_blk // 2) + slot) * PACKED, PACKED)

    def late_tile(at):
        packed = x[pl.ds(at + block, half), :].astype(F32)
        return packed, pltpu.roll(packed, LANES // 2, 1)

    @pl.when(j == 0)
    def _():
        live = count[lax.axis_index("band")]

        def fill(own, at, cols, used):
            lane = lax.broadcasted_iota(jnp.int32, own.shape, 1)
            slot = lane & 7
            turned = jnp.where(
                (lane & 8) == 0, pltpu.roll(own, LANES - 8, 1), -pltpu.roll(own, 8, 1)
            )
            keep = (slot < live) & (lane < used)
            own, turned = jnp.where(keep, own, 0.0), jnp.where(keep, turned, 0.0)
            for s in range(SLOTS):
                for part, value in ((0, own), (1, turned)):
                    to = (part * SLOTS + s) * block + at
                    lhs[to : to + own.shape[0], cols] = jnp.where(slot == s, value, 0.0).astype(BF16)

        mine = rows_of(b)
        fill(x[pl.ds(mine, block), :].astype(F32), 0, slice(0, LANES), LANES)
        for n, part in enumerate(late_tile(mine)):
            fill(part, n * half, slice(LANES, 2 * LANES), (NSPEC - 8) * 16)

    low = lax.broadcasted_iota(jnp.int32, (half, LANES), 1) < LANES // 2
    for n in range(COLUMNS // block):
        at = rows_of(j * (COLUMNS // block) + n)
        right[n * block : (n + 1) * block, :LANES] = x[pl.ds(at, block), :]
        for m, part in enumerate(late_tile(at)):
            to = n * block + m * half
            right[to : to + half, LANES:] = jnp.where(low, part, 0.0).astype(BF16)
    y = lax.dot_general(
        lhs[...], right[...], (((1,), (1,)), ((), ())), preferred_element_type=F32
    )
    y = (y * (1.0 / NSPEC)).astype(BF16)
    for part in range(2):
        for s in range(SLOTS):
            at = (part * SLOTS + s) * block
            out[part, 0, s] = y[at : at + block]


def correlate(x, count, n_band, n_blk):
    block = EL * n_band
    everyone = block * n_blk

    def body(*refs):
        correlate_kernel(n_blk, *refs)

    return pl.pallas_call(
        body,
        grid=(everyone // COLUMNS,),
        out_shape=jax.ShapeDtypeStruct((2, 1, SLOTS, block, everyone), BF16),
        in_specs=[
            pl.BlockSpec(memory_space=pltpu.VMEM),
            pl.BlockSpec(memory_space=pltpu.SMEM),
        ],
        out_specs=pl.BlockSpec((2, 1, SLOTS, block, COLUMNS), lambda j: (0, 0, 0, 0, j)),
        scratch_shapes=[
            pltpu.VMEM((2 * SLOTS * block, 2 * LANES), BF16),
            pltpu.VMEM((COLUMNS, 2 * LANES), BF16),
        ],
        compiler_params=pltpu.CompilerParams(vmem_limit_bytes=32 * 2**20),
        name="correlate",
    )(x, count)


def solution(mesh):
    n_band, n_blk = mesh.shape["band"], mesh.shape["blk"]

    def local(volt, band_chans, band_count):
        x = front(volt, band_chans, n_band, n_blk)
        return correlate(x, band_count, n_band, n_blk)

    return jax.shard_map(
        local,
        mesh=mesh,
        in_specs=(P(None, ("blk", "band"), None), P(), P()),
        out_specs=P(None, "band", None, "blk", None),
        check_vma=False,
    )
```

```python
import math

import jax
import jax.numpy as jnp
import numpy as np
from jax import lax
from jax.experimental import pallas as pl
from jax.experimental.pallas import tpu as pltpu
from jax.sharding import PartitionSpec as P

C = 4096
TAPS = 16
NSPEC = 12
FRAMES = NSPEC + TAPS - 1
EL = 16
LANES = 128
BANDS = 8
SLOTS = 8
GROUPS = 4
GROUP_W = C // GROUPS
CHUNK = 512
N_CENTRE = 4
N_CHUNK = C // CHUNK
MESH = pl.DeviceIdType.MESH
F32, BF16 = jnp.float32, jnp.bfloat16


def taper_scale():
    idx = np.arange(TAPS * C, dtype=np.float64)
    centre = (idx + 0.5) / C - TAPS / 2.0
    window = 0.5 - 0.5 * np.cos(2.0 * math.pi * (idx + 0.5) / (TAPS * C))
    prototype = np.sinc(centre) * window
    return float(1.0 / np.sqrt(np.sum(prototype * prototype)))


def half_sine(x):
    y = jnp.minimum(x, math.pi - x)
    y2 = y * y
    s = 1.0 / 120 + y2 * (-1.0 / 5040 + y2 * (1.0 / 362880 + y2 * (-1.0 / 39916800)))
    return y * (1.0 + y2 * (-1.0 / 6 + y2 * s))


def fill_taper(taper):
    width = 512
    scale = taper_scale() / math.pi

    def some(n, carry):
        tap = lax.broadcasted_iota(jnp.int32, (TAPS, width), 0)
        k = lax.broadcasted_iota(jnp.int32, (TAPS, width), 1) + n * width
        frac = (k.astype(F32) + 0.5) * (1.0 / C)
        top = half_sine(frac * math.pi) * jnp.where((tap & 1) == 0, scale, -scale)
        window = half_sine((tap.astype(F32) + frac) * (math.pi / TAPS))
        value = top * window * window / (frac + (tap - TAPS // 2).astype(F32))
        taper[:, pl.ds(pl.multiple_of(n * width, width), width)] = value
        return carry

    lax.fori_loop(0, C // width, some, 0)


def cos_sin(turns):
    shifted = turns + 512
    quarter = (shifted >> 10) & 3
    x = ((shifted & 1023) - 512).astype(F32) * (2.0 * math.pi / 4096.0)
    x2 = x * x
    s = x * (1.0 + x2 * (-1.0 / 6 + x2 * (1.0 / 120 + x2 * (-1.0 / 5040 + x2 * (1.0 / 362880)))))
    c = 1.0 + x2 * (-0.5 + x2 * (1.0 / 24 + x2 * (-1.0 / 720 + x2 * (1.0 / 40320))))
    odd = (quarter & 1) == 1
    cc, ss = jnp.where(odd, s, c), jnp.where(odd, c, s)
    cc = jnp.where((quarter == 1) | (quarter == 2), -cc, cc)
    ss = jnp.where(quarter >= 2, -ss, ss)
    return cc, ss


def split(y):
    hi = y.astype(BF16)
    return hi, (y - hi.astype(F32)).astype(BF16)


CENTRE = tuple(range(TAPS // 2 - N_CENTRE // 2, TAPS // 2 + N_CENTRE // 2))
OUTER = tuple(p for p in range(TAPS) if p not in CENTRE)
ROWS = 2 * NSPEC * EL


def front_kernel(
    n_band, n_blk, volt, chans_hbm, left, right, chans, taper, small_sem, samples, base_c, base_s,
    step_c, step_s, table, lhs_a, lhs_b, total, sems, z, turned, x, *comm_sems
):
    def fetch(group, frame):
        return pltpu.make_async_copy(
            volt.at[:, :, pl.ds(frame * C + group * GROUP_W, GROUP_W)],
            samples.at[group, frame],
            sems.at[group],
        )

    def fetch_group(group):
        for frame in range(FRAMES):
            fetch(group, frame).start()

    small = pltpu.make_async_copy(chans_hbm, chans, small_sem.at[0])
    small.start()
    fetch_group(0)
    greet(n_band, n_blk)
    fetch_group(1)
    fill_taper(taper)
    small.wait()

    lane = lax.broadcasted_iota(jnp.int32, (8, LANES), 1)
    key = ((lane >> 4) << 3) + (lane & 7)
    row = jnp.zeros((8, LANES), jnp.int32)
    for g in range(BANDS):
        for s in range(SLOTS):
            row = jnp.where(key == g * SLOTS + s, chans[g, s], row)
    quarter_turn = ((lane[:1] >> 3) & 1) * 1024
    row = row[:1]
    inner = lax.broadcasted_iota(jnp.int32, (LANES, LANES), 0)
    c0, s0 = cos_sin((inner * row + quarter_turn) & 4095)
    base_c[...] = c0
    base_s[...] = s0
    outer = lax.broadcasted_iota(jnp.int32, (C // LANES, LANES), 0) * LANES
    c1, s1 = cos_sin((outer * row) & 4095)
    step_c[...] = c1
    step_s[...] = s1

    def build(chunk, carry):
        for part in range(CHUNK // LANES):
            a = chunk * (CHUNK // LANES) + part
            ca, sa = step_c[pl.ds(a, 1), :], step_s[pl.ds(a, 1), :]
            hi, lo = split(ca * base_c[...] - sa * base_s[...])
            rows = slice(part * LANES, (part + 1) * LANES)
            table[chunk, rows, :LANES] = hi
            table[chunk, rows, LANES:] = lo
        return carry

    lax.fori_loop(0, N_CHUNK, build, 0)

    def weigh(chunk, lhs):
        group = chunk // (GROUP_W // CHUNK)
        for part in range(CHUNK // LANES):
            k = pl.multiple_of(chunk * CHUNK + part * LANES, LANES)
            in_group = pl.multiple_of(k - group * GROUP_W, LANES)
            taps = [
                jnp.broadcast_to(taper[p : p + 1, pl.ds(k, LANES)], (EL, LANES))
                for p in range(TAPS)
            ]
            taps = [taps[p] if p in CENTRE else taps[p].astype(BF16) for p in range(TAPS)]
            column = slice(part * LANES, (part + 1) * LANES)
            for comp in range(2):
                side, mid = [None] * NSPEC, [None] * NSPEC
                for f in range(FRAMES):
                    x = samples[group, f, comp, :, pl.ds(in_group, LANES)]
                    wide = x.astype(F32)
                    for t in range(max(0, f - TAPS + 1), min(NSPEC - 1, f) + 1):
                        p = f - t
                        if p in CENTRE:
                            term = taps[p] * wide
                            mid[t] = term if mid[t] is None else mid[t] + term
                        else:
                            term = taps[p] * x
                            side[t] = term if side[t] is None else side[t] + term
                    if f >= TAPS - 1:
                        t = f - TAPS + 1
                        hi, lo = split(mid[t] + side[t].astype(F32))
                        at = (comp * NSPEC + t) * EL
                        lhs[at : at + EL, column] = hi
                        lhs[ROWS + at : ROWS + at + EL, column] = lo

    def transform(chunk, lhs):
        r = jnp.dot(lhs[...], table[chunk], preferred_element_type=F32)
        total[...] += (r[:ROWS, LANES:] + r[ROWS:, :LANES]) + r[:ROWS, :LANES]

    def wait_group(group):
        pltpu.make_async_copy(samples.at[group], samples.at[group], sems.at[group]).wait()

    total[...] = jnp.zeros_like(total)
    lhs_b[...] = jnp.zeros_like(lhs_b)

    per_group = GROUP_W // CHUNK

    def two_chunks(i, carry):
        first = i * 2
        weigh(first, lhs_a)
        transform(lax.max(first - 1, 0), lhs_b)
        weigh(first + 1, lhs_b)
        transform(first, lhs_a)
        return carry

    for group in range(GROUPS):
        if group + 2 < GROUPS:
            fetch_group(group + 2)
        wait_group(group)
        lax.fori_loop(group * per_group // 2, (group + 1) * per_group // 2, two_chunks, 0)
    transform(N_CHUNK - 1, lhs_b)

    is_real = (lax.broadcasted_iota(jnp.int32, (EL, LANES), 1) & 8) == 0
    y = []
    for t in range(NSPEC):
        re = total[t * EL : (t + 1) * EL, :]
        im = total[(NSPEC + t) * EL : (NSPEC + t + 1) * EL, :]
        swapped = jnp.where(is_real, -pltpu.roll(im, LANES - 8, 1), pltpu.roll(im, 8, 1))
        y.append(re + swapped)
    place = lax.broadcasted_iota(jnp.int32, (EL, LANES), 1) >> 4
    for g in range(BANDS):
        for tile in range(2):
            out = jnp.zeros((EL, LANES), F32)
            for t in range(tile * 8, min(tile * 8 + 8, NSPEC)):
                moved = y[t]
                shift = (t - g) * 16 % LANES
                if shift:
                    moved = pltpu.roll(moved, shift, 1)
                out = jnp.where(place == t - tile * 8, moved, out)
            z[g, :, tile * LANES : (tile + 1) * LANES] = out.astype(BF16)
    share(n_band, n_blk, z, turned, x, chans, left, right, *comm_sems)


def places(n_band, n_blk):
    g, b = lax.axis_index("band"), lax.axis_index("blk")
    core, near, along = b % 2, b // 2 % 2, b // 4
    n_along = n_blk // 4

    def chip(d_along, d_near):
        return ((along + d_along + n_along) % n_along * 2 + (near + d_near) % 2) * 2 + core

    return g, b, b + 1 - 2 * core, chip


STEPS = ((1, 0), (-1, 1), (-1, 0), (1, 1), (0, 1))
PASSED = (0, 1)


NEARBY = ((0, 0), (0, 1), (1, 0), (1, 1), (-1, 0), (-1, 1), (2, 0), (2, 1))


def slot_of(d_along, d_near):
    return NEARBY.index(((d_along + 1) % 4 - 1, d_near))


PACKED = 192


def greet(n_band, n_blk):
    g, b, sibling, chip = places(n_band, n_blk)
    peers = [((g + d) % n_band, b) for d in range(1, n_band)]
    peers += [(g, chip(*step)) for step in STEPS] + [(g, sibling)]
    barrier = pltpu.get_barrier_semaphore()
    for peer in peers:
        pl.semaphore_signal(barrier, inc=1, device_id=peer, device_id_type=MESH)


def fill_left(left, turned, live):
    block = turned.shape[0]
    for tile in range(2):
        cols = slice(tile * LANES, (tile + 1) * LANES)
        own = turned[:, cols].astype(F32)
        lane = lax.broadcasted_iota(jnp.int32, own.shape, 1)
        slot = lane & 7
        crossed = jnp.where(
            (lane & 8) == 0, pltpu.roll(own, LANES - 8, 1), -pltpu.roll(own, 8, 1)
        )
        own, crossed = jnp.where(slot < live, own, 0.0), jnp.where(slot < live, crossed, 0.0)
        for s in range(SLOTS):
            for part, value in ((0, own), (1, crossed)):
                at = (part * SLOTS + s) * block
                left[at : at + block, cols] = jnp.where(slot == s, value, 0.0).astype(BF16)


def share(
    n_band, n_blk, z, turned, x, chans, left, right, ct_send, ct_recv, ag_send, ag_recv, fw_send,
    fw_recv, here,
):
    g, b, sibling, chip = places(n_band, n_blk)
    pl.semaphore_wait(pltpu.get_barrier_semaphore(), n_band - 1 + len(STEPS) + 1)
    block = EL * n_band
    half = block // 2
    core = b % 2
    low = lax.broadcasted_iota(jnp.int32, (half, LANES), 1) < LANES // 2

    def slots(of_core, start, count=1):
        at = pl.multiple_of((of_core * (n_blk // 2) + start) * PACKED, PACKED)
        return x.at[pl.ds(at, count * PACKED)]

    def remote(src, dst, send, recv, to):
        copy = pltpu.make_async_remote_copy(src, dst, send, recv, to, MESH)
        copy.start()
        return copy

    def unpack(of_core, first, count):
        for slot in range(first, first + count):
            owner = chip(*NEARBY[slot]) - core + of_core
            at = pl.multiple_of(owner * block, block)
            kept = slots(of_core, slot)
            right[pl.ds(at, block), :LANES] = kept[:block, :]
            packed = kept[block:, :].astype(F32)
            for n, part in enumerate((packed, pltpu.roll(packed, LANES // 2, 1))):
                part = jnp.where(low, part, 0.0).astype(BF16)
                right[pl.ds(pl.multiple_of(at + n * half, half), half), LANES:] = part

    mine = turned.at[pl.ds(pl.multiple_of(g * EL, EL), EL)]
    turns = []
    for d in range(1, n_band):
        to = (g + d) % n_band
        turns.append(remote(z.at[to], mine, ct_send.at[d], ct_recv.at[d], (to, b)))
    keep = pltpu.make_async_copy(z.at[g], mine, here.at[0])
    keep.start()
    keep.wait()
    for turn in turns:
        turn.wait_recv()
    own = slots(core, 0)
    top = turned[:half, LANES:].astype(F32)
    bottom = pltpu.roll(turned[half:, LANES:].astype(F32), LANES // 2, 1)
    own[:block, :] = turned[:, :LANES]
    own[block:, :] = jnp.where(low, top, bottom).astype(BF16)

    sends = [
        remote(own, slots(core, slot_of(-da, dn)), ag_send.at[n], ag_recv.at[n], (g, chip(da, dn)))
        for n, (da, dn) in enumerate(STEPS)
    ]
    fill_left(left, turned, chans[BANDS, g])
    unpack(core, 0, 1)
    onward = []
    for n, (da, dn) in enumerate(STEPS):
        sends[n].wait_recv()
        if n in PASSED:
            m = len(STEPS) + len(onward)
            came, goes = slots(core, slot_of(-da, dn)), slots(core, slot_of(-2 * da, dn))
            onward.append(remote(came, goes, ag_send.at[m], ag_recv.at[m], (g, chip(da, 0))))
    n_near = len(STEPS) + 1
    near, far = slots(core, 0, n_near), slots(core, n_near, 2)
    near_copy = remote(near, near, fw_send.at[0], fw_recv.at[0], (g, sibling))
    unpack(core, 1, n_near - 1)
    near_copy.wait_recv()
    unpack(1 - core, 0, n_near)
    for copy in onward:
        copy.wait_recv()
    far_copy = remote(far, far, fw_send.at[1], fw_recv.at[1], (g, sibling))
    unpack(core, n_near, 2)
    far_copy.wait_recv()
    unpack(1 - core, n_near, 2)
    for copy in turns + sends + onward + [near_copy, far_copy]:
        copy.wait_send()


def front(volt, chans, n_band, n_blk):
    hbm = pl.BlockSpec(memory_space=pltpu.HBM)
    dma = pltpu.SemaphoreType.DMA
    n_copies = len(STEPS) + len(PASSED)
    vmem = pl.BlockSpec(memory_space=pltpu.VMEM)

    def body(*refs):
        front_kernel(n_band, n_blk, *refs)

    return pl.pallas_call(
        body,
        out_shape=[
            jax.ShapeDtypeStruct((2 * SLOTS * EL * n_band, 2 * LANES), BF16),
            jax.ShapeDtypeStruct((EL * n_band * n_blk, 2 * LANES), BF16),
        ],
        in_specs=[hbm] * 2,
        out_specs=[vmem] * 2,
        scratch_shapes=[
            pltpu.SMEM((BANDS + 1, SLOTS), jnp.int32),
            pltpu.VMEM((TAPS, C), F32),
            dma((1,)),
            pltpu.VMEM((GROUPS, FRAMES, 2, EL, GROUP_W), BF16),
            pltpu.VMEM((LANES, LANES), F32),
            pltpu.VMEM((LANES, LANES), F32),
            pltpu.VMEM((C // LANES, LANES), F32),
            pltpu.VMEM((C // LANES, LANES), F32),
            pltpu.VMEM((N_CHUNK, CHUNK, 2 * LANES), BF16),
            pltpu.VMEM((2 * ROWS, CHUNK), BF16),
            pltpu.VMEM((2 * ROWS, CHUNK), BF16),
            pltpu.VMEM((ROWS, LANES), F32),
            dma((GROUPS,)),
            pltpu.VMEM((BANDS, EL, 2 * LANES), BF16),
            pltpu.VMEM((EL * n_band, 2 * LANES), BF16),
            pltpu.VMEM((n_blk * PACKED, LANES), BF16),
            dma((n_band,)),
            dma((n_band,)),
            dma((n_copies,)),
            dma((n_copies,)),
            dma((2,)),
            dma((2,)),
            dma((1,)),
        ],
        compiler_params=pltpu.CompilerParams(
            vmem_limit_bytes=48 * 2**20, collective_id=0, has_side_effects=True
        ),
        name="spectra",
    )(volt, chans)


COLUMNS = 512


def correlate_kernel(left, right, out):
    j, part = pl.program_id(0), pl.program_id(1)
    block = out.shape[3]
    rows = SLOTS * block
    y = lax.dot_general(
        left[pl.ds(pl.multiple_of(part * rows, rows), rows), :],
        right[pl.ds(pl.multiple_of(j * COLUMNS, COLUMNS), COLUMNS), :],
        (((1,), (1,)), ((), ())),
        preferred_element_type=F32,
    )
    y = (y * (1.0 / NSPEC)).astype(BF16)
    for s in range(SLOTS):
        out[0, 0, s] = y[s * block : (s + 1) * block]


def correlate(left, right):
    block, everyone = left.shape[0] // (2 * SLOTS), right.shape[0]
    vmem = pl.BlockSpec(memory_space=pltpu.VMEM)
    return pl.pallas_call(
        correlate_kernel,
        grid=(everyone // COLUMNS, 2),
        out_shape=jax.ShapeDtypeStruct((2, 1, SLOTS, block, everyone), BF16),
        in_specs=[vmem, vmem],
        out_specs=pl.BlockSpec(
            (1, 1, SLOTS, block, COLUMNS), lambda j, part: (part, 0, 0, 0, j)
        ),
        compiler_params=pltpu.CompilerParams(vmem_limit_bytes=32 * 2**20),
        name="correlate",
    )(left, right)


def solution(mesh):
    n_band, n_blk = mesh.shape["band"], mesh.shape["blk"]

    def local(volt, band_chans, band_count):
        small = jnp.concatenate([band_chans, band_count[None]])
        left, right = front(volt, small, n_band, n_blk)
        return correlate(left, right)

    return jax.shard_map(
        local,
        mesh=mesh,
        in_specs=(P(None, ("blk", "band"), None), P(), P()),
        out_specs=P(None, "band", None, "blk", None),
        check_vma=False,
    )
```

```python
import math

import jax
import jax.numpy as jnp
import numpy as np
from jax import lax
from jax.experimental import pallas as pl
from jax.experimental.pallas import tpu as pltpu
from jax.sharding import PartitionSpec as P

C = 4096
TAPS = 16
NSPEC = 12
FRAMES = NSPEC + TAPS - 1
EL = 16
LANES = 128
BANDS = 8
SLOTS = 8
GROUPS = 4
GROUP_W = C // GROUPS
CHUNK = 512
N_CENTRE = 2
N_CHUNK = C // CHUNK
MESH = pl.DeviceIdType.MESH
F32, BF16 = jnp.float32, jnp.bfloat16


def taper_scale():
    idx = np.arange(TAPS * C, dtype=np.float64)
    centre = (idx + 0.5) / C - TAPS / 2.0
    window = 0.5 - 0.5 * np.cos(2.0 * math.pi * (idx + 0.5) / (TAPS * C))
    prototype = np.sinc(centre) * window
    return float(1.0 / np.sqrt(np.sum(prototype * prototype)))


def half_sine(x):
    y = jnp.minimum(x, math.pi - x)
    y2 = y * y
    s = 1.0 / 120 + y2 * (-1.0 / 5040 + y2 * (1.0 / 362880 + y2 * (-1.0 / 39916800)))
    return y * (1.0 + y2 * (-1.0 / 6 + y2 * s))


def fill_taper(taper):
    width = 512
    scale = taper_scale() / math.pi

    def some(n, carry):
        tap = lax.broadcasted_iota(jnp.int32, (TAPS, width), 0)
        k = lax.broadcasted_iota(jnp.int32, (TAPS, width), 1) + n * width
        frac = (k.astype(F32) + 0.5) * (1.0 / C)
        top = half_sine(frac * math.pi) * jnp.where((tap & 1) == 0, scale, -scale)
        window = half_sine((tap.astype(F32) + frac) * (math.pi / TAPS))
        value = top * window * window / (frac + (tap - TAPS // 2).astype(F32))
        taper[:, pl.ds(pl.multiple_of(n * width, width), width)] = value
        return carry

    lax.fori_loop(0, C // width, some, 0)


def cos_sin(turns):
    shifted = turns + 512
    quarter = (shifted >> 10) & 3
    x = ((shifted & 1023) - 512).astype(F32) * (2.0 * math.pi / 4096.0)
    x2 = x * x
    s = x * (1.0 + x2 * (-1.0 / 6 + x2 * (1.0 / 120 + x2 * (-1.0 / 5040 + x2 * (1.0 / 362880)))))
    c = 1.0 + x2 * (-0.5 + x2 * (1.0 / 24 + x2 * (-1.0 / 720 + x2 * (1.0 / 40320))))
    odd = (quarter & 1) == 1
    cc, ss = jnp.where(odd, s, c), jnp.where(odd, c, s)
    cc = jnp.where((quarter == 1) | (quarter == 2), -cc, cc)
    ss = jnp.where(quarter >= 2, -ss, ss)
    return cc, ss


def split(y):
    hi = y.astype(BF16)
    return hi, (y - hi.astype(F32)).astype(BF16)


CENTRE = tuple(range(TAPS // 2 - N_CENTRE // 2, TAPS // 2 + N_CENTRE // 2))
OUTER = tuple(p for p in range(TAPS) if p not in CENTRE)
ROWS = 2 * NSPEC * EL


def front_kernel(
    n_band, n_blk, volt, chans_hbm, left, right, chans, taper, small_sem, samples, base_c, base_s,
    step_c, step_s, table, lhs_a, lhs_b, total, sems, z, turned, x, *comm_sems
):
    def fetch(group, frame):
        return pltpu.make_async_copy(
            volt.at[:, :, pl.ds(frame * C + group * GROUP_W, GROUP_W)],
            samples.at[group, frame],
            sems.at[group],
        )

    def fetch_group(group):
        for frame in range(FRAMES):
            fetch(group, frame).start()

    small = pltpu.make_async_copy(chans_hbm, chans, small_sem.at[0])
    small.start()
    fetch_group(0)
    greet(n_band, n_blk)
    fetch_group(1)
    fill_taper(taper)
    small.wait()

    lane = lax.broadcasted_iota(jnp.int32, (8, LANES), 1)
    key = ((lane >> 4) << 3) + (lane & 7)
    row = jnp.zeros((8, LANES), jnp.int32)
    for g in range(BANDS):
        for s in range(SLOTS):
            row = jnp.where(key == g * SLOTS + s, chans[g, s], row)
    quarter_turn = ((lane[:1] >> 3) & 1) * 1024
    row = row[:1]
    inner = lax.broadcasted_iota(jnp.int32, (LANES, LANES), 0)
    c0, s0 = cos_sin((inner * row + quarter_turn) & 4095)
    base_c[...] = c0
    base_s[...] = s0
    outer = lax.broadcasted_iota(jnp.int32, (C // LANES, LANES), 0) * LANES
    c1, s1 = cos_sin((outer * row) & 4095)
    step_c[...] = c1
    step_s[...] = s1

    def build(chunk, carry):
        for part in range(CHUNK // LANES):
            a = chunk * (CHUNK // LANES) + part
            ca, sa = step_c[pl.ds(a, 1), :], step_s[pl.ds(a, 1), :]
            hi, lo = split(ca * base_c[...] - sa * base_s[...])
            rows = slice(part * LANES, (part + 1) * LANES)
            table[chunk, rows, :LANES] = hi
            table[chunk, rows, LANES:] = lo
        return carry

    lax.fori_loop(0, N_CHUNK, build, 0)

    def weigh(chunk, lhs, before=None):
        group = chunk // (GROUP_W // CHUNK)
        for part in range(CHUNK // LANES):
            k = pl.multiple_of(chunk * CHUNK + part * LANES, LANES)
            in_group = pl.multiple_of(k - group * GROUP_W, LANES)
            taps = [
                jnp.broadcast_to(taper[p : p + 1, pl.ds(k, LANES)], (EL, LANES))
                for p in range(TAPS)
            ]
            taps = [taps[p] if p in CENTRE else taps[p].astype(BF16) for p in range(TAPS)]
            column = slice(part * LANES, (part + 1) * LANES)
            if before is not None:
                piece(before[0], before[1], part)
            for comp in range(2):
                side, mid = [None] * NSPEC, [None] * NSPEC
                for f in range(FRAMES):
                    x = samples[group, f, comp, :, pl.ds(in_group, LANES)]
                    wide = x.astype(F32)
                    for t in range(max(0, f - TAPS + 1), min(NSPEC - 1, f) + 1):
                        p = f - t
                        if p in CENTRE:
                            term = taps[p] * wide
                            mid[t] = term if mid[t] is None else mid[t] + term
                        else:
                            term = taps[p] * x
                            side[t] = term if side[t] is None else side[t] + term
                    if f >= TAPS - 1:
                        t = f - TAPS + 1
                        hi, lo = split(mid[t] + side[t].astype(F32))
                        at = (comp * NSPEC + t) * EL
                        lhs[at : at + EL, column] = hi
                        lhs[ROWS + at : ROWS + at + EL, column] = lo

    def piece(chunk, lhs, n):
        count = ROWS // 2
        at = n * count
        if n < 2:
            r = jnp.dot(lhs[at : at + count, :], table[chunk], preferred_element_type=F32)
            total[at : at + count, :] += r[:, :LANES] + r[:, LANES:]
        else:
            r = jnp.dot(lhs[at : at + count, :], table[chunk, :, :LANES], preferred_element_type=F32)
            total[at - ROWS : at - ROWS + count, :] += r

    def wait_group(group):
        pltpu.make_async_copy(samples.at[group], samples.at[group], sems.at[group]).wait()

    total[...] = jnp.zeros_like(total)
    lhs_b[...] = jnp.zeros_like(lhs_b)

    per_group = GROUP_W // CHUNK

    def two_chunks(i, carry):
        first = i * 2
        weigh(first, lhs_a, (lax.max(first - 1, 0), lhs_b))
        weigh(first + 1, lhs_b, (first, lhs_a))
        return carry

    for group in range(GROUPS):
        if group + 2 < GROUPS:
            fetch_group(group + 2)
        wait_group(group)
        lax.fori_loop(group * per_group // 2, (group + 1) * per_group // 2, two_chunks, 0)
    for n in range(4):
        piece(N_CHUNK - 1, lhs_b, n)

    is_real = (lax.broadcasted_iota(jnp.int32, (EL, LANES), 1) & 8) == 0
    y = []
    for t in range(NSPEC):
        re = total[t * EL : (t + 1) * EL, :]
        im = total[(NSPEC + t) * EL : (NSPEC + t + 1) * EL, :]
        swapped = jnp.where(is_real, -pltpu.roll(im, LANES - 8, 1), pltpu.roll(im, 8, 1))
        y.append(re + swapped)
    place = lax.broadcasted_iota(jnp.int32, (EL, LANES), 1) >> 4
    for g in range(BANDS):
        for tile in range(2):
            out = jnp.zeros((EL, LANES), F32)
            for t in range(tile * 8, min(tile * 8 + 8, NSPEC)):
                moved = y[t]
                shift = (t - g) * 16 % LANES
                if shift:
                    moved = pltpu.roll(moved, shift, 1)
                out = jnp.where(place == t - tile * 8, moved, out)
            z[g, :, tile * LANES : (tile + 1) * LANES] = out.astype(BF16)
    share(n_band, n_blk, z, turned, x, chans, left, right, *comm_sems)


def places(n_band, n_blk):
    g, b = lax.axis_index("band"), lax.axis_index("blk")
    core, near, along = b % 2, b // 2 % 2, b // 4
    n_along = n_blk // 4

    def chip(d_along, d_near):
        return ((along + d_along + n_along) % n_along * 2 + (near + d_near) % 2) * 2 + core

    return g, b, b + 1 - 2 * core, chip


STEPS = ((1, 0), (-1, 1), (-1, 0), (1, 1), (0, 1))
PASSED = (0, 1)


NEARBY = ((0, 0), (0, 1), (1, 0), (1, 1), (-1, 0), (-1, 1), (2, 0), (2, 1))


def slot_of(d_along, d_near):
    return NEARBY.index(((d_along + 1) % 4 - 1, d_near))


PACKED = 192


def greet(n_band, n_blk):
    g, b, sibling, chip = places(n_band, n_blk)
    peers = [((g + d) % n_band, b) for d in range(1, n_band)]
    peers += [(g, chip(*step)) for step in STEPS] + [(g, sibling)]
    barrier = pltpu.get_barrier_semaphore()
    for peer in peers:
        pl.semaphore_signal(barrier, inc=1, device_id=peer, device_id_type=MESH)


def fill_left(left, turned, live):
    block = turned.shape[0]
    for tile in range(2):
        cols = slice(tile * LANES, (tile + 1) * LANES)
        own = turned[:, cols].astype(F32)
        lane = lax.broadcasted_iota(jnp.int32, own.shape, 1)
        slot = lane & 7
        crossed = jnp.where(
            (lane & 8) == 0, pltpu.roll(own, LANES - 8, 1), -pltpu.roll(own, 8, 1)
        )
        own, crossed = jnp.where(slot < live, own, 0.0), jnp.where(slot < live, crossed, 0.0)
        for s in range(SLOTS):
            for part, value in ((0, own), (1, crossed)):
                at = (part * SLOTS + s) * block
                left[at : at + block, cols] = jnp.where(slot == s, value, 0.0).astype(BF16)


def share(
    n_band, n_blk, z, turned, x, chans, left, right, ct_send, ct_recv, ag_send, ag_recv, fw_send,
    fw_recv, here,
):
    g, b, sibling, chip = places(n_band, n_blk)
    pl.semaphore_wait(pltpu.get_barrier_semaphore(), n_band - 1 + len(STEPS) + 1)
    block = EL * n_band
    half = block // 2
    core = b % 2
    low = lax.broadcasted_iota(jnp.int32, (half, LANES), 1) < LANES // 2

    def slots(of_core, start, count=1):
        at = pl.multiple_of((of_core * (n_blk // 2) + start) * PACKED, PACKED)
        return x.at[pl.ds(at, count * PACKED)]

    def remote(src, dst, send, recv, to):
        copy = pltpu.make_async_remote_copy(src, dst, send, recv, to, MESH)
        copy.start()
        return copy

    def unpack(of_core, first, count):
        for slot in range(first, first + count):
            owner = chip(*NEARBY[slot]) - core + of_core
            at = pl.multiple_of(owner * block, block)
            kept = slots(of_core, slot)
            right[pl.ds(at, block), :LANES] = kept[:block, :]
            packed = kept[block:, :].astype(F32)
            for n, part in enumerate((packed, pltpu.roll(packed, LANES // 2, 1))):
                part = jnp.where(low, part, 0.0).astype(BF16)
                right[pl.ds(pl.multiple_of(at + n * half, half), half), LANES:] = part

    mine = turned.at[pl.ds(pl.multiple_of(g * EL, EL), EL)]
    turns = []
    for d in range(1, n_band):
        to = (g + d) % n_band
        turns.append(remote(z.at[to], mine, ct_send.at[d], ct_recv.at[d], (to, b)))
    keep = pltpu.make_async_copy(z.at[g], mine, here.at[0])
    keep.start()
    keep.wait()
    for turn in turns:
        turn.wait_recv()
    own = slots(core, 0)
    top = turned[:half, LANES:].astype(F32)
    bottom = pltpu.roll(turned[half:, LANES:].astype(F32), LANES // 2, 1)
    own[:block, :] = turned[:, :LANES]
    own[block:, :] = jnp.where(low, top, bottom).astype(BF16)

    sends = [
        remote(own, slots(core, slot_of(-da, dn)), ag_send.at[n], ag_recv.at[n], (g, chip(da, dn)))
        for n, (da, dn) in enumerate(STEPS)
    ]
    fill_left(left, turned, chans[BANDS, g])
    unpack(core, 0, 1)
    onward = []
    for n, (da, dn) in enumerate(STEPS):
        sends[n].wait_recv()
        if n in PASSED:
            m = len(STEPS) + len(onward)
            came, goes = slots(core, slot_of(-da, dn)), slots(core, slot_of(-2 * da, dn))
            onward.append(remote(came, goes, ag_send.at[m], ag_recv.at[m], (g, chip(da, 0))))
    n_near = len(STEPS) + 1
    near, far = slots(core, 0, n_near), slots(core, n_near, 2)
    near_copy = remote(near, near, fw_send.at[0], fw_recv.at[0], (g, sibling))
    unpack(core, 1, n_near - 1)
    near_copy.wait_recv()
    unpack(1 - core, 0, n_near)
    for copy in onward:
        copy.wait_recv()
    far_copy = remote(far, far, fw_send.at[1], fw_recv.at[1], (g, sibling))
    unpack(core, n_near, 2)
    far_copy.wait_recv()
    unpack(1 - core, n_near, 2)
    for copy in turns + sends + onward + [near_copy, far_copy]:
        copy.wait_send()


def front(volt, chans, n_band, n_blk):
    hbm = pl.BlockSpec(memory_space=pltpu.HBM)
    dma = pltpu.SemaphoreType.DMA
    n_copies = len(STEPS) + len(PASSED)
    vmem = pl.BlockSpec(memory_space=pltpu.VMEM)

    def body(*refs):
        front_kernel(n_band, n_blk, *refs)

    return pl.pallas_call(
        body,
        out_shape=[
            jax.ShapeDtypeStruct((2 * SLOTS * EL * n_band, 2 * LANES), BF16),
            jax.ShapeDtypeStruct((EL * n_band * n_blk, 2 * LANES), BF16),
        ],
        in_specs=[hbm] * 2,
        out_specs=[vmem] * 2,
        scratch_shapes=[
            pltpu.SMEM((BANDS + 1, SLOTS), jnp.int32),
            pltpu.VMEM((TAPS, C), F32),
            dma((1,)),
            pltpu.VMEM((GROUPS, FRAMES, 2, EL, GROUP_W), BF16),
            pltpu.VMEM((LANES, LANES), F32),
            pltpu.VMEM((LANES, LANES), F32),
            pltpu.VMEM((C // LANES, LANES), F32),
            pltpu.VMEM((C // LANES, LANES), F32),
            pltpu.VMEM((N_CHUNK, CHUNK, 2 * LANES), BF16),
            pltpu.VMEM((2 * ROWS, CHUNK), BF16),
            pltpu.VMEM((2 * ROWS, CHUNK), BF16),
            pltpu.VMEM((ROWS, LANES), F32),
            dma((GROUPS,)),
            pltpu.VMEM((BANDS, EL, 2 * LANES), BF16),
            pltpu.VMEM((EL * n_band, 2 * LANES), BF16),
            pltpu.VMEM((n_blk * PACKED, LANES), BF16),
            dma((n_band,)),
            dma((n_band,)),
            dma((n_copies,)),
            dma((n_copies,)),
            dma((2,)),
            dma((2,)),
            dma((1,)),
        ],
        compiler_params=pltpu.CompilerParams(
            vmem_limit_bytes=48 * 2**20, collective_id=0, has_side_effects=True
        ),
        name="spectra",
    )(volt, chans)


COLUMNS = 512


def correlate_kernel(left, right, out, done, sems):
    block = out.shape[3]
    everyone = right.shape[0]
    copies = []
    for at in range(0, everyone, COLUMNS):
        cols = slice(at, at + COLUMNS)
        for first, last in ((0, 4), (4, 8), (8, 16)) if at == 0 else ((0, 8), (8, 16)):
            y = lax.dot_general(
                left[first * block : last * block, :],
                right[cols, :],
                (((1,), (1,)), ((), ())),
                preferred_element_type=F32,
            )
            y = (y * (1.0 / NSPEC)).astype(BF16)
            for n in range(first, last):
                part, s = n // SLOTS, n % SLOTS
                done[part, s, :, cols] = y[(n - first) * block : (n - first + 1) * block]
                if n % 2:
                    pair = pl.ds(s - 1, 2)
                    copies.append(
                        pltpu.make_async_copy(
                            done.at[part, pair, :, pl.ds(at, COLUMNS)],
                            out.at[part, 0, pair, :, pl.ds(at, COLUMNS)],
                            sems.at[len(copies)],
                        )
                    )
                    copies[-1].start()
    for copy in copies:
        copy.wait()


def correlate(left, right):
    block, everyone = left.shape[0] // (2 * SLOTS), right.shape[0]
    vmem = pl.BlockSpec(memory_space=pltpu.VMEM)
    return pl.pallas_call(
        correlate_kernel,
        out_shape=jax.ShapeDtypeStruct((2, 1, SLOTS, block, everyone), BF16),
        in_specs=[vmem, vmem],
        out_specs=pl.BlockSpec(memory_space=pltpu.HBM),
        scratch_shapes=[
            pltpu.VMEM((2, SLOTS, block, everyone), BF16),
            pltpu.SemaphoreType.DMA((SLOTS * everyone // COLUMNS,)),
        ],
        compiler_params=pltpu.CompilerParams(vmem_limit_bytes=48 * 2**20),
        name="correlate",
    )(left, right)


def solution(mesh):
    n_band, n_blk = mesh.shape["band"], mesh.shape["blk"]

    def local(volt, band_chans, band_count):
        small = jnp.concatenate([band_chans, band_count[None]])
        left, right = front(volt, small, n_band, n_blk)
        return correlate(left, right)

    return jax.shard_map(
        local,
        mesh=mesh,
        in_specs=(P(None, ("blk", "band"), None), P(), P()),
        out_specs=P(None, "band", None, "blk", None),
        check_vma=False,
    )
```

```python
import math

import jax
import jax.numpy as jnp
import numpy as np
from jax import lax
from jax.experimental import pallas as pl
from jax.experimental.pallas import tpu as pltpu
from jax.sharding import PartitionSpec as P

C = 4096
TAPS = 16
NSPEC = 12
FRAMES = NSPEC + TAPS - 1
EL = 16
LANES = 128
BANDS = 8
SLOTS = 8
GROUPS = 4
GROUP_W = C // GROUPS
CHUNK = 512
N_CENTRE = 2
N_CHUNK = C // CHUNK
MESH = pl.DeviceIdType.MESH
F32, BF16 = jnp.float32, jnp.bfloat16


def taper_scale():
    idx = np.arange(TAPS * C, dtype=np.float64)
    centre = (idx + 0.5) / C - TAPS / 2.0
    window = 0.5 - 0.5 * np.cos(2.0 * math.pi * (idx + 0.5) / (TAPS * C))
    prototype = np.sinc(centre) * window
    return float(1.0 / np.sqrt(np.sum(prototype * prototype)))


def half_sine(x):
    y = jnp.minimum(x, math.pi - x)
    y2 = y * y
    s = 1.0 / 120 + y2 * (-1.0 / 5040 + y2 * (1.0 / 362880 + y2 * (-1.0 / 39916800)))
    return y * (1.0 + y2 * (-1.0 / 6 + y2 * s))


def fill_taper(taper):
    width = 512
    scale = taper_scale() / math.pi

    def some(n, carry):
        tap = lax.broadcasted_iota(jnp.int32, (TAPS, width), 0)
        k = lax.broadcasted_iota(jnp.int32, (TAPS, width), 1) + n * width
        frac = (k.astype(F32) + 0.5) * (1.0 / C)
        top = half_sine(frac * math.pi) * jnp.where((tap & 1) == 0, scale, -scale)
        window = half_sine((tap.astype(F32) + frac) * (math.pi / TAPS))
        value = top * window * window / (frac + (tap - TAPS // 2).astype(F32))
        taper[:, pl.ds(pl.multiple_of(n * width, width), width)] = value
        return carry

    lax.fori_loop(0, C // width, some, 0)


def cos_sin(turns):
    shifted = turns + 512
    quarter = (shifted >> 10) & 3
    x = ((shifted & 1023) - 512).astype(F32) * (2.0 * math.pi / 4096.0)
    x2 = x * x
    s = x * (1.0 + x2 * (-1.0 / 6 + x2 * (1.0 / 120 + x2 * (-1.0 / 5040 + x2 * (1.0 / 362880)))))
    c = 1.0 + x2 * (-0.5 + x2 * (1.0 / 24 + x2 * (-1.0 / 720 + x2 * (1.0 / 40320))))
    odd = (quarter & 1) == 1
    cc, ss = jnp.where(odd, s, c), jnp.where(odd, c, s)
    cc = jnp.where((quarter == 1) | (quarter == 2), -cc, cc)
    ss = jnp.where(quarter >= 2, -ss, ss)
    return cc, ss


def split(y):
    hi = y.astype(BF16)
    return hi, (y - hi.astype(F32)).astype(BF16)


CENTRE = tuple(range(TAPS // 2 - N_CENTRE // 2, TAPS // 2 + N_CENTRE // 2))
OUTER = tuple(p for p in range(TAPS) if p not in CENTRE)
ROWS = 2 * NSPEC * EL


def front_kernel(
    n_band, n_blk, volt, chans_hbm, count_hbm, left, right, chans, count, taper, small_sem, samples, base_c, base_s,
    step_c, step_s, table, lhs_a, lhs_b, total, sems, z, turned, x, *comm_sems
):
    def fetch(group, frame):
        return pltpu.make_async_copy(
            volt.at[:, :, pl.ds(frame * C + group * GROUP_W, GROUP_W)],
            samples.at[group, frame],
            sems.at[group],
        )

    def fetch_group(group):
        for frame in range(FRAMES):
            fetch(group, frame).start()

    small = [
        pltpu.make_async_copy(chans_hbm, chans, small_sem.at[0]),
        pltpu.make_async_copy(count_hbm, count, small_sem.at[1]),
    ]
    for copy in small:
        copy.start()
    fetch_group(0)
    greet(n_band, n_blk)
    fetch_group(1)
    fill_taper(taper)
    for copy in small:
        copy.wait()

    lane = lax.broadcasted_iota(jnp.int32, (8, LANES), 1)
    key = ((lane >> 4) << 3) + (lane & 7)
    row = jnp.zeros((8, LANES), jnp.int32)
    for g in range(BANDS):
        for s in range(SLOTS):
            row = jnp.where(key == g * SLOTS + s, chans[g, s], row)
    quarter_turn = ((lane[:1] >> 3) & 1) * 1024
    row = row[:1]
    inner = lax.broadcasted_iota(jnp.int32, (LANES, LANES), 0)
    c0, s0 = cos_sin((inner * row + quarter_turn) & 4095)
    base_c[...] = c0
    base_s[...] = s0
    outer = lax.broadcasted_iota(jnp.int32, (C // LANES, LANES), 0) * LANES
    c1, s1 = cos_sin((outer * row) & 4095)
    step_c[...] = c1
    step_s[...] = s1

    def build(chunk, carry):
        for part in range(CHUNK // LANES):
            a = chunk * (CHUNK // LANES) + part
            ca, sa = step_c[pl.ds(a, 1), :], step_s[pl.ds(a, 1), :]
            hi, lo = split(ca * base_c[...] - sa * base_s[...])
            rows = slice(part * LANES, (part + 1) * LANES)
            table[chunk, rows, :LANES] = hi
            table[chunk, rows, LANES:] = lo
        return carry

    lax.fori_loop(0, N_CHUNK, build, 0)

    def weigh(chunk, lhs, before=None):
        group = chunk // (GROUP_W // CHUNK)
        for part in range(CHUNK // LANES):
            k = pl.multiple_of(chunk * CHUNK + part * LANES, LANES)
            in_group = pl.multiple_of(k - group * GROUP_W, LANES)
            taps = [
                jnp.broadcast_to(taper[p : p + 1, pl.ds(k, LANES)], (EL, LANES))
                for p in range(TAPS)
            ]
            taps = [taps[p] if p in CENTRE else taps[p].astype(BF16) for p in range(TAPS)]
            column = slice(part * LANES, (part + 1) * LANES)
            if before is not None:
                piece(before[0], before[1], part)
            for comp in range(2):
                x = [samples[group, f, comp, :, pl.ds(in_group, LANES)] for f in range(FRAMES)]
                for t in range(NSPEC):
                    sides = []
                    for order in (OUTER[: len(OUTER) // 2], OUTER[: len(OUTER) // 2 - 1 : -1]):
                        side = taps[order[0]] * x[t + order[0]]
                        for p in order[1:]:
                            side = side + taps[p] * x[t + p]
                        sides.append(side)
                    y = sides[0].astype(F32) + sides[1].astype(F32)
                    for p in CENTRE:
                        y = y + taps[p] * x[t + p].astype(F32)
                    hi, lo = split(y)
                    at = (comp * NSPEC + t) * EL
                    lhs[at : at + EL, column] = hi
                    lhs[ROWS + at : ROWS + at + EL, column] = lo

    def piece(chunk, lhs, n):
        count = ROWS // 2
        at = n * count
        if n < 2:
            r = jnp.dot(lhs[at : at + count, :], table[chunk], preferred_element_type=F32)
            total[at : at + count, :] += r[:, :LANES] + r[:, LANES:]
        else:
            r = jnp.dot(lhs[at : at + count, :], table[chunk, :, :LANES], preferred_element_type=F32)
            total[at - ROWS : at - ROWS + count, :] += r

    def wait_group(group):
        pltpu.make_async_copy(samples.at[group], samples.at[group], sems.at[group]).wait()

    total[...] = jnp.zeros_like(total)
    lhs_b[...] = jnp.zeros_like(lhs_b)

    per_group = GROUP_W // CHUNK

    def two_chunks(i, carry):
        first = i * 2
        weigh(first, lhs_a, (lax.max(first - 1, 0), lhs_b))
        weigh(first + 1, lhs_b, (first, lhs_a))
        return carry

    for group in range(GROUPS):
        if group + 2 < GROUPS:
            fetch_group(group + 2)
        wait_group(group)
        lax.fori_loop(group * per_group // 2, (group + 1) * per_group // 2, two_chunks, 0)
    for n in range(4):
        piece(N_CHUNK - 1, lhs_b, n)

    is_real = (lax.broadcasted_iota(jnp.int32, (EL, LANES), 1) & 8) == 0
    y = []
    for t in range(NSPEC):
        re = total[t * EL : (t + 1) * EL, :]
        im = total[(NSPEC + t) * EL : (NSPEC + t + 1) * EL, :]
        swapped = jnp.where(is_real, -pltpu.roll(im, LANES - 8, 1), pltpu.roll(im, 8, 1))
        y.append(re + swapped)
    place = lax.broadcasted_iota(jnp.int32, (EL, LANES), 1) >> 4
    for g in range(BANDS):
        for tile in range(2):
            out = jnp.zeros((EL, LANES), F32)
            for t in range(tile * 8, min(tile * 8 + 8, NSPEC)):
                moved = y[t]
                shift = (t - g) * 16 % LANES
                if shift:
                    moved = pltpu.roll(moved, shift, 1)
                out = jnp.where(place == t - tile * 8, moved, out)
            z[g, :, tile * LANES : (tile + 1) * LANES] = out.astype(BF16)
    share(n_band, n_blk, z, turned, x, count, left, right, *comm_sems)


def places(n_band, n_blk):
    g, b = lax.axis_index("band"), lax.axis_index("blk")
    core, near, along = b % 2, b // 2 % 2, b // 4
    n_along = n_blk // 4

    def chip(d_along, d_near):
        return ((along + d_along + n_along) % n_along * 2 + (near + d_near) % 2) * 2 + core

    return g, b, b + 1 - 2 * core, chip


STEPS = ((1, 0), (-1, 1), (-1, 0), (1, 1), (0, 1))
PASSED = (0, 1)


NEARBY = ((0, 0), (0, 1), (1, 0), (1, 1), (-1, 0), (-1, 1), (2, 0), (2, 1))


def slot_of(d_along, d_near):
    return NEARBY.index(((d_along + 1) % 4 - 1, d_near))


PACKED = 192


def greet(n_band, n_blk):
    g, b, sibling, chip = places(n_band, n_blk)
    peers = [((g + d) % n_band, b) for d in range(1, n_band)]
    peers += [(g, chip(*step)) for step in STEPS] + [(g, sibling)]
    barrier = pltpu.get_barrier_semaphore()
    for peer in peers:
        pl.semaphore_signal(barrier, inc=1, device_id=peer, device_id_type=MESH)


def fill_left(left, turned, live):
    block = turned.shape[0]
    for tile in range(2):
        cols = slice(tile * LANES, (tile + 1) * LANES)
        own = turned[:, cols].astype(F32)
        lane = lax.broadcasted_iota(jnp.int32, own.shape, 1)
        slot = lane & 7
        crossed = jnp.where(
            (lane & 8) == 0, pltpu.roll(own, LANES - 8, 1), -pltpu.roll(own, 8, 1)
        )
        own, crossed = jnp.where(slot < live, own, 0.0), jnp.where(slot < live, crossed, 0.0)
        for s in range(SLOTS):
            for part, value in ((0, own), (1, crossed)):
                at = (part * SLOTS + s) * block
                left[at : at + block, cols] = jnp.where(slot == s, value, 0.0).astype(BF16)


def share(
    n_band, n_blk, z, turned, x, count, left, right, ct_send, ct_recv, ag_send, ag_recv, fw_send,
    fw_recv, here,
):
    g, b, sibling, chip = places(n_band, n_blk)
    pl.semaphore_wait(pltpu.get_barrier_semaphore(), n_band - 1 + len(STEPS) + 1)
    block = EL * n_band
    half = block // 2
    core = b % 2
    low = lax.broadcasted_iota(jnp.int32, (half, LANES), 1) < LANES // 2

    def slots(of_core, start, count=1):
        at = pl.multiple_of((of_core * (n_blk // 2) + start) * PACKED, PACKED)
        return x.at[pl.ds(at, count * PACKED)]

    def remote(src, dst, send, recv, to):
        copy = pltpu.make_async_remote_copy(src, dst, send, recv, to, MESH)
        copy.start()
        return copy

    def unpack(of_core, first, count):
        for slot in range(first, first + count):
            owner = chip(*NEARBY[slot]) - core + of_core
            at = pl.multiple_of(owner * block, block)
            kept = slots(of_core, slot)
            right[pl.ds(at, block), :LANES] = kept[:block, :]
            packed = kept[block:, :].astype(F32)
            for n, part in enumerate((packed, pltpu.roll(packed, LANES // 2, 1))):
                part = jnp.where(low, part, 0.0).astype(BF16)
                right[pl.ds(pl.multiple_of(at + n * half, half), half), LANES:] = part

    mine = turned.at[pl.ds(pl.multiple_of(g * EL, EL), EL)]
    turns = []
    for d in range(1, n_band):
        to = (g + d) % n_band
        turns.append(remote(z.at[to], mine, ct_send.at[d], ct_recv.at[d], (to, b)))
    keep = pltpu.make_async_copy(z.at[g], mine, here.at[0])
    keep.start()
    keep.wait()
    for turn in turns:
        turn.wait_recv()
    own = slots(core, 0)
    top = turned[:half, LANES:].astype(F32)
    bottom = pltpu.roll(turned[half:, LANES:].astype(F32), LANES // 2, 1)
    own[:block, :] = turned[:, :LANES]
    own[block:, :] = jnp.where(low, top, bottom).astype(BF16)

    sends = [
        remote(own, slots(core, slot_of(-da, dn)), ag_send.at[n], ag_recv.at[n], (g, chip(da, dn)))
        for n, (da, dn) in enumerate(STEPS)
    ]
    fill_left(left, turned, count[g])
    unpack(core, 0, 1)
    onward = []
    for n, (da, dn) in enumerate(STEPS):
        sends[n].wait_recv()
        if n in PASSED:
            m = len(STEPS) + len(onward)
            came, goes = slots(core, slot_of(-da, dn)), slots(core, slot_of(-2 * da, dn))
            onward.append(remote(came, goes, ag_send.at[m], ag_recv.at[m], (g, chip(da, 0))))
    n_near = len(STEPS) + 1
    near, far = slots(core, 0, n_near), slots(core, n_near, 2)
    near_copy = remote(near, near, fw_send.at[0], fw_recv.at[0], (g, sibling))
    unpack(core, 1, n_near - 1)
    near_copy.wait_recv()
    unpack(1 - core, 0, n_near)
    for copy in onward:
        copy.wait_recv()
    far_copy = remote(far, far, fw_send.at[1], fw_recv.at[1], (g, sibling))
    unpack(core, n_near, 2)
    far_copy.wait_recv()
    unpack(1 - core, n_near, 2)
    for copy in turns + sends + onward + [near_copy, far_copy]:
        copy.wait_send()


def front(volt, chans, count, n_band, n_blk):
    hbm = pl.BlockSpec(memory_space=pltpu.HBM)
    dma = pltpu.SemaphoreType.DMA
    n_copies = len(STEPS) + len(PASSED)
    vmem = pl.BlockSpec(memory_space=pltpu.VMEM)

    def body(*refs):
        front_kernel(n_band, n_blk, *refs)

    return pl.pallas_call(
        body,
        out_shape=[
            jax.ShapeDtypeStruct((2 * SLOTS * EL * n_band, 2 * LANES), BF16),
            jax.ShapeDtypeStruct((EL * n_band * n_blk, 2 * LANES), BF16),
        ],
        in_specs=[hbm] * 3,
        out_specs=[vmem] * 2,
        scratch_shapes=[
            pltpu.SMEM((BANDS, SLOTS), jnp.int32),
            pltpu.SMEM((BANDS,), jnp.int32),
            pltpu.VMEM((TAPS, C), F32),
            dma((2,)),
            pltpu.VMEM((GROUPS, FRAMES, 2, EL, GROUP_W), BF16),
            pltpu.VMEM((LANES, LANES), F32),
            pltpu.VMEM((LANES, LANES), F32),
            pltpu.VMEM((C // LANES, LANES), F32),
            pltpu.VMEM((C // LANES, LANES), F32),
            pltpu.VMEM((N_CHUNK, CHUNK, 2 * LANES), BF16),
            pltpu.VMEM((2 * ROWS, CHUNK), BF16),
            pltpu.VMEM((2 * ROWS, CHUNK), BF16),
            pltpu.VMEM((ROWS, LANES), F32),
            dma((GROUPS,)),
            pltpu.VMEM((BANDS, EL, 2 * LANES), BF16),
            pltpu.VMEM((EL * n_band, 2 * LANES), BF16),
            pltpu.VMEM((n_blk * PACKED, LANES), BF16),
            dma((n_band,)),
            dma((n_band,)),
            dma((n_copies,)),
            dma((n_copies,)),
            dma((2,)),
            dma((2,)),
            dma((1,)),
        ],
        compiler_params=pltpu.CompilerParams(
            vmem_limit_bytes=48 * 2**20, collective_id=0, has_side_effects=True
        ),
        name="spectra",
    )(volt, chans, count)


COLUMNS = 512


def correlate_kernel(left, right, out, done, sems):
    block = out.shape[3]
    everyone = right.shape[0]
    copies = []
    for at in range(0, everyone, COLUMNS):
        cols = slice(at, at + COLUMNS)
        for first, last in ((0, 4), (4, 8), (8, 16)) if at == 0 else ((0, 8), (8, 16)):
            y = lax.dot_general(
                left[first * block : last * block, :],
                right[cols, :],
                (((1,), (1,)), ((), ())),
                preferred_element_type=F32,
            )
            y = (y * (1.0 / NSPEC)).astype(BF16)
            for n in range(first, last):
                part, s = n // SLOTS, n % SLOTS
                done[part, s, :, cols] = y[(n - first) * block : (n - first + 1) * block]
                if n % 2:
                    pair = pl.ds(s - 1, 2)
                    copies.append(
                        pltpu.make_async_copy(
                            done.at[part, pair, :, pl.ds(at, COLUMNS)],
                            out.at[part, 0, pair, :, pl.ds(at, COLUMNS)],
                            sems.at[len(copies)],
                        )
                    )
                    copies[-1].start()
    for copy in copies:
        copy.wait()


def correlate(left, right):
    block, everyone = left.shape[0] // (2 * SLOTS), right.shape[0]
    vmem = pl.BlockSpec(memory_space=pltpu.VMEM)
    return pl.pallas_call(
        correlate_kernel,
        out_shape=jax.ShapeDtypeStruct((2, 1, SLOTS, block, everyone), BF16),
        in_specs=[vmem, vmem],
        out_specs=pl.BlockSpec(memory_space=pltpu.HBM),
        scratch_shapes=[
            pltpu.VMEM((2, SLOTS, block, everyone), BF16),
            pltpu.SemaphoreType.DMA((SLOTS * everyone // COLUMNS,)),
        ],
        compiler_params=pltpu.CompilerParams(vmem_limit_bytes=48 * 2**20),
        name="correlate",
    )(left, right)


def solution(mesh):
    n_band, n_blk = mesh.shape["band"], mesh.shape["blk"]

    def local(volt, band_chans, band_count):
        chans, count = (
            pltpu.with_memory_space_constraint(a, pltpu.HBM) for a in (band_chans, band_count)
        )
        left, right = front(volt, chans, count, n_band, n_blk)
        return correlate(left, right)

    return jax.shard_map(
        local,
        mesh=mesh,
        in_specs=(P(None, ("blk", "band"), None), P(), P()),
        out_specs=P(None, "band", None, "blk", None),
        check_vma=False,
    )
```

```python
import math

import jax
import jax.numpy as jnp
import numpy as np
from jax import lax
from jax.experimental import pallas as pl
from jax.experimental.pallas import tpu as pltpu
from jax.sharding import PartitionSpec as P

C = 4096
TAPS = 16
NSPEC = 12
FRAMES = NSPEC + TAPS - 1
EL = 16
LANES = 128
BANDS = 8
SLOTS = 8
GROUPS = 4
GROUP_W = C // GROUPS
CHUNK = 512
N_CENTRE = 2
N_CHUNK = C // CHUNK
MESH = pl.DeviceIdType.MESH
F32, BF16 = jnp.float32, jnp.bfloat16


def taper_scale():
    idx = np.arange(TAPS * C, dtype=np.float64)
    centre = (idx + 0.5) / C - TAPS / 2.0
    window = 0.5 - 0.5 * np.cos(2.0 * math.pi * (idx + 0.5) / (TAPS * C))
    prototype = np.sinc(centre) * window
    return float(1.0 / np.sqrt(np.sum(prototype * prototype)))


def half_sine(x):
    y = jnp.minimum(x, math.pi - x)
    y2 = y * y
    s = 1.0 / 120 + y2 * (-1.0 / 5040 + y2 * (1.0 / 362880 + y2 * (-1.0 / 39916800)))
    return y * (1.0 + y2 * (-1.0 / 6 + y2 * s))


def fill_taper(taper):
    width = 512
    scale = taper_scale() / math.pi

    def some(n, carry):
        tap = lax.broadcasted_iota(jnp.int32, (TAPS, width), 0)
        k = lax.broadcasted_iota(jnp.int32, (TAPS, width), 1) + n * width
        frac = (k.astype(F32) + 0.5) * (1.0 / C)
        top = half_sine(frac * math.pi) * jnp.where((tap & 1) == 0, scale, -scale)
        window = half_sine((tap.astype(F32) + frac) * (math.pi / TAPS))
        value = top * window * window / (frac + (tap - TAPS // 2).astype(F32))
        taper[:, pl.ds(pl.multiple_of(n * width, width), width)] = value
        return carry

    lax.fori_loop(0, C // width, some, 0)


def cos_sin(turns):
    shifted = turns + 512
    quarter = (shifted >> 10) & 3
    x = ((shifted & 1023) - 512).astype(F32) * (2.0 * math.pi / 4096.0)
    x2 = x * x
    s = x * (1.0 + x2 * (-1.0 / 6 + x2 * (1.0 / 120 + x2 * (-1.0 / 5040 + x2 * (1.0 / 362880)))))
    c = 1.0 + x2 * (-0.5 + x2 * (1.0 / 24 + x2 * (-1.0 / 720 + x2 * (1.0 / 40320))))
    odd = (quarter & 1) == 1
    cc, ss = jnp.where(odd, s, c), jnp.where(odd, c, s)
    cc = jnp.where((quarter == 1) | (quarter == 2), -cc, cc)
    ss = jnp.where(quarter >= 2, -ss, ss)
    return cc, ss


def split(y):
    hi = y.astype(BF16)
    return hi, (y - hi.astype(F32)).astype(BF16)


CENTRE = tuple(range(TAPS // 2 - N_CENTRE // 2, TAPS // 2 + N_CENTRE // 2))
OUTER = tuple(p for p in range(TAPS) if p not in CENTRE)
ROWS = 2 * NSPEC * EL


def front_kernel(
    n_band, n_blk, volt, chans_hbm, count_hbm, left, right, chans, count, taper, small_sem, samples, base_c, base_s,
    step_c, step_s, table, lhs_a, lhs_b, total, sems, z, turned, x, *comm_sems
):
    def fetch(group, frame):
        return pltpu.make_async_copy(
            volt.at[:, :, pl.ds(frame * C + group * GROUP_W, GROUP_W)],
            samples.at[group, frame],
            sems.at[group],
        )

    def fetch_group(group):
        for frame in range(FRAMES):
            fetch(group, frame).start()

    small = [
        pltpu.make_async_copy(chans_hbm, chans, small_sem.at[0]),
        pltpu.make_async_copy(count_hbm, count, small_sem.at[1]),
    ]
    for copy in small:
        copy.start()
    fetch_group(0)
    greet(n_band, n_blk)
    fetch_group(1)
    fill_taper(taper)
    for copy in small:
        copy.wait()

    lane = lax.broadcasted_iota(jnp.int32, (8, LANES), 1)
    key = ((lane >> 4) << 3) + (lane & 7)
    row = jnp.zeros((8, LANES), jnp.int32)
    for g in range(BANDS):
        for s in range(SLOTS):
            row = jnp.where(key == g * SLOTS + s, chans[g, s], row)
    quarter_turn = ((lane[:1] >> 3) & 1) * 1024
    row = row[:1]
    inner = lax.broadcasted_iota(jnp.int32, (LANES, LANES), 0)
    c0, s0 = cos_sin((inner * row + quarter_turn) & 4095)
    base_c[...] = c0
    base_s[...] = s0
    outer = lax.broadcasted_iota(jnp.int32, (C // LANES, LANES), 0) * LANES
    c1, s1 = cos_sin((outer * row) & 4095)
    step_c[...] = c1
    step_s[...] = s1

    def build(chunk, carry):
        for part in range(CHUNK // LANES):
            a = chunk * (CHUNK // LANES) + part
            ca, sa = step_c[pl.ds(a, 1), :], step_s[pl.ds(a, 1), :]
            hi, lo = split(ca * base_c[...] - sa * base_s[...])
            rows = slice(part * LANES, (part + 1) * LANES)
            table[chunk, rows, :LANES] = hi
            table[chunk, rows, LANES:] = lo
        return carry

    lax.fori_loop(0, N_CHUNK, build, 0)

    def weigh(chunk, lhs, before=None):
        group = chunk // (GROUP_W // CHUNK)
        for part in range(CHUNK // LANES):
            k = chunk * CHUNK + part * LANES
            in_group = k - group * GROUP_W
            taps = [
                jnp.broadcast_to(taper[p : p + 1, pl.ds(k, LANES)], (EL, LANES))
                for p in range(TAPS)
            ]
            taps = [taps[p] if p in CENTRE else taps[p].astype(BF16) for p in range(TAPS)]
            column = slice(part * LANES, (part + 1) * LANES)
            if before is not None:
                piece(before[0], before[1], part)
            for comp in range(2):
                x = [samples[group, f, comp, :, pl.ds(in_group, LANES)] for f in range(FRAMES)]
                for t in range(NSPEC):
                    sides = []
                    for order in (OUTER[: len(OUTER) // 2], OUTER[: len(OUTER) // 2 - 1 : -1]):
                        side = taps[order[0]] * x[t + order[0]]
                        for p in order[1:]:
                            side = side + taps[p] * x[t + p]
                        sides.append(side)
                    y = sides[0].astype(F32) + sides[1].astype(F32)
                    for p in CENTRE:
                        y = y + taps[p] * x[t + p].astype(F32)
                    hi, lo = split(y)
                    at = (comp * NSPEC + t) * EL
                    lhs[at : at + EL, column] = hi
                    lhs[ROWS + at : ROWS + at + EL, column] = lo

    def piece(chunk, lhs, n):
        count = ROWS // 2
        at = n * count
        if n < 2:
            r = jnp.dot(lhs[at : at + count, :], table[chunk], preferred_element_type=F32)
            total[at : at + count, :] += r[:, :LANES] + r[:, LANES:]
        else:
            r = jnp.dot(lhs[at : at + count, :], table[chunk, :, :LANES], preferred_element_type=F32)
            total[at - ROWS : at - ROWS + count, :] += r

    def wait_group(group):
        pltpu.make_async_copy(samples.at[group], samples.at[group], sems.at[group]).wait()

    total[...] = jnp.zeros_like(total)
    per_group = GROUP_W // CHUNK
    held, other, before = lhs_a, lhs_b, None
    for chunk in range(N_CHUNK):
        if chunk % per_group == 0:
            group = chunk // per_group
            if group + 2 < GROUPS:
                fetch_group(group + 2)
            wait_group(group)
        weigh(chunk, held, before)
        before = (chunk, held)
        held, other = other, held
    for n in range(4):
        piece(*before, n)

    is_real = (lax.broadcasted_iota(jnp.int32, (EL, LANES), 1) & 8) == 0
    y = []
    for t in range(NSPEC):
        re = total[t * EL : (t + 1) * EL, :]
        im = total[(NSPEC + t) * EL : (NSPEC + t + 1) * EL, :]
        swapped = jnp.where(is_real, -pltpu.roll(im, LANES - 8, 1), pltpu.roll(im, 8, 1))
        y.append(re + swapped)
    place = lax.broadcasted_iota(jnp.int32, (EL, LANES), 1) >> 4
    for g in range(BANDS):
        for tile in range(2):
            out = jnp.zeros((EL, LANES), F32)
            for t in range(tile * 8, min(tile * 8 + 8, NSPEC)):
                moved = y[t]
                shift = (t - g) * 16 % LANES
                if shift:
                    moved = pltpu.roll(moved, shift, 1)
                out = jnp.where(place == t - tile * 8, moved, out)
            z[g, :, tile * LANES : (tile + 1) * LANES] = out.astype(BF16)
    share(n_band, n_blk, z, turned, x, count, left, right, *comm_sems)


def places(n_band, n_blk):
    g, b = lax.axis_index("band"), lax.axis_index("blk")
    core, near, along = b % 2, b // 2 % 2, b // 4
    n_along = n_blk // 4

    def chip(d_along, d_near):
        return ((along + d_along + n_along) % n_along * 2 + (near + d_near) % 2) * 2 + core

    return g, b, b + 1 - 2 * core, chip


STEPS = ((1, 0), (-1, 1), (-1, 0), (1, 1), (0, 1))
PASSED = (0, 1)


NEARBY = ((0, 0), (0, 1), (1, 0), (1, 1), (-1, 0), (-1, 1), (2, 0), (2, 1))


def slot_of(d_along, d_near):
    return NEARBY.index(((d_along + 1) % 4 - 1, d_near))


PACKED = 192


def greet(n_band, n_blk):
    g, b, sibling, chip = places(n_band, n_blk)
    peers = [((g + d) % n_band, b) for d in range(1, n_band)]
    peers += [(g, chip(*step)) for step in STEPS] + [(g, sibling)]
    barrier = pltpu.get_barrier_semaphore()
    for peer in peers:
        pl.semaphore_signal(barrier, inc=1, device_id=peer, device_id_type=MESH)


def fill_left(left, turned, live):
    block = turned.shape[0]
    for tile in range(2):
        cols = slice(tile * LANES, (tile + 1) * LANES)
        own = turned[:, cols].astype(F32)
        lane = lax.broadcasted_iota(jnp.int32, own.shape, 1)
        slot = lane & 7
        crossed = jnp.where(
            (lane & 8) == 0, pltpu.roll(own, LANES - 8, 1), -pltpu.roll(own, 8, 1)
        )
        own, crossed = jnp.where(slot < live, own, 0.0), jnp.where(slot < live, crossed, 0.0)
        for s in range(SLOTS):
            for part, value in ((0, own), (1, crossed)):
                at = (part * SLOTS + s) * block
                left[at : at + block, cols] = jnp.where(slot == s, value, 0.0).astype(BF16)


def share(
    n_band, n_blk, z, turned, x, count, left, right, ct_send, ct_recv, ag_send, ag_recv, fw_send,
    fw_recv, here,
):
    g, b, sibling, chip = places(n_band, n_blk)
    pl.semaphore_wait(pltpu.get_barrier_semaphore(), n_band - 1 + len(STEPS) + 1)
    block = EL * n_band
    half = block // 2
    core = b % 2
    low = lax.broadcasted_iota(jnp.int32, (half, LANES), 1) < LANES // 2

    def slots(of_core, start, count=1):
        at = pl.multiple_of((of_core * (n_blk // 2) + start) * PACKED, PACKED)
        return x.at[pl.ds(at, count * PACKED)]

    def remote(src, dst, send, recv, to):
        copy = pltpu.make_async_remote_copy(src, dst, send, recv, to, MESH)
        copy.start()
        return copy

    def unpack(of_core, first, count):
        for slot in range(first, first + count):
            owner = chip(*NEARBY[slot]) - core + of_core
            at = pl.multiple_of(owner * block, block)
            kept = slots(of_core, slot)
            right[pl.ds(at, block), :LANES] = kept[:block, :]
            packed = kept[block:, :].astype(F32)
            for n, part in enumerate((packed, pltpu.roll(packed, LANES // 2, 1))):
                part = jnp.where(low, part, 0.0).astype(BF16)
                right[pl.ds(pl.multiple_of(at + n * half, half), half), LANES:] = part

    mine = turned.at[pl.ds(pl.multiple_of(g * EL, EL), EL)]
    turns = []
    for d in range(1, n_band):
        to = (g + d) % n_band
        turns.append(remote(z.at[to], mine, ct_send.at[d], ct_recv.at[d], (to, b)))
    keep = pltpu.make_async_copy(z.at[g], mine, here.at[0])
    keep.start()
    keep.wait()
    for turn in turns:
        turn.wait_recv()
    own = slots(core, 0)
    top = turned[:half, LANES:].astype(F32)
    bottom = pltpu.roll(turned[half:, LANES:].astype(F32), LANES // 2, 1)
    own[:block, :] = turned[:, :LANES]
    own[block:, :] = jnp.where(low, top, bottom).astype(BF16)

    sends = [
        remote(own, slots(core, slot_of(-da, dn)), ag_send.at[n], ag_recv.at[n], (g, chip(da, dn)))
        for n, (da, dn) in enumerate(STEPS)
    ]
    fill_left(left, turned, count[g])
    unpack(core, 0, 1)
    onward = []
    for n, (da, dn) in enumerate(STEPS):
        sends[n].wait_recv()
        if n in PASSED:
            m = len(STEPS) + len(onward)
            came, goes = slots(core, slot_of(-da, dn)), slots(core, slot_of(-2 * da, dn))
            onward.append(remote(came, goes, ag_send.at[m], ag_recv.at[m], (g, chip(da, 0))))
    n_near = len(STEPS) + 1
    near, far = slots(core, 0, n_near), slots(core, n_near, 2)
    near_copy = remote(near, near, fw_send.at[0], fw_recv.at[0], (g, sibling))
    unpack(core, 1, n_near - 1)
    near_copy.wait_recv()
    unpack(1 - core, 0, n_near)
    for copy in onward:
        copy.wait_recv()
    far_copy = remote(far, far, fw_send.at[1], fw_recv.at[1], (g, sibling))
    unpack(core, n_near, 2)
    far_copy.wait_recv()
    unpack(1 - core, n_near, 2)
    for copy in turns + sends + onward + [near_copy, far_copy]:
        copy.wait_send()


def front(volt, chans, count, n_band, n_blk):
    hbm = pl.BlockSpec(memory_space=pltpu.HBM)
    dma = pltpu.SemaphoreType.DMA
    n_copies = len(STEPS) + len(PASSED)
    vmem = pl.BlockSpec(memory_space=pltpu.VMEM)

    def body(*refs):
        front_kernel(n_band, n_blk, *refs)

    return pl.pallas_call(
        body,
        out_shape=[
            jax.ShapeDtypeStruct((2 * SLOTS * EL * n_band, 2 * LANES), BF16),
            jax.ShapeDtypeStruct((EL * n_band * n_blk, 2 * LANES), BF16),
        ],
        in_specs=[hbm] * 3,
        out_specs=[vmem] * 2,
        scratch_shapes=[
            pltpu.SMEM((BANDS, SLOTS), jnp.int32),
            pltpu.SMEM((BANDS,), jnp.int32),
            pltpu.VMEM((TAPS, C), F32),
            dma((2,)),
            pltpu.VMEM((GROUPS, FRAMES, 2, EL, GROUP_W), BF16),
            pltpu.VMEM((LANES, LANES), F32),
            pltpu.VMEM((LANES, LANES), F32),
            pltpu.VMEM((C // LANES, LANES), F32),
            pltpu.VMEM((C // LANES, LANES), F32),
            pltpu.VMEM((N_CHUNK, CHUNK, 2 * LANES), BF16),
            pltpu.VMEM((2 * ROWS, CHUNK), BF16),
            pltpu.VMEM((2 * ROWS, CHUNK), BF16),
            pltpu.VMEM((ROWS, LANES), F32),
            dma((GROUPS,)),
            pltpu.VMEM((BANDS, EL, 2 * LANES), BF16),
            pltpu.VMEM((EL * n_band, 2 * LANES), BF16),
            pltpu.VMEM((n_blk * PACKED, LANES), BF16),
            dma((n_band,)),
            dma((n_band,)),
            dma((n_copies,)),
            dma((n_copies,)),
            dma((2,)),
            dma((2,)),
            dma((1,)),
        ],
        compiler_params=pltpu.CompilerParams(
            vmem_limit_bytes=48 * 2**20, collective_id=0, has_side_effects=True
        ),
        name="spectra",
    )(volt, chans, count)


COLUMNS = 512


def correlate_kernel(left, right, out, done, sems):
    block = out.shape[3]
    everyone = right.shape[0]
    copies = []
    for at in range(0, everyone, COLUMNS):
        cols = slice(at, at + COLUMNS)
        for first, last in ((0, 4), (4, 8), (8, 16)) if at == 0 else ((0, 8), (8, 16)):
            y = lax.dot_general(
                left[first * block : last * block, :],
                right[cols, :],
                (((1,), (1,)), ((), ())),
                preferred_element_type=F32,
            )
            y = (y * (1.0 / NSPEC)).astype(BF16)
            for n in range(first, last):
                part, s = n // SLOTS, n % SLOTS
                done[part, s, :, cols] = y[(n - first) * block : (n - first + 1) * block]
                if n % 2:
                    pair = pl.ds(s - 1, 2)
                    copies.append(
                        pltpu.make_async_copy(
                            done.at[part, pair, :, pl.ds(at, COLUMNS)],
                            out.at[part, 0, pair, :, pl.ds(at, COLUMNS)],
                            sems.at[len(copies)],
                        )
                    )
                    copies[-1].start()
    for copy in copies:
        copy.wait()


def correlate(left, right):
    block, everyone = left.shape[0] // (2 * SLOTS), right.shape[0]
    vmem = pl.BlockSpec(memory_space=pltpu.VMEM)
    return pl.pallas_call(
        correlate_kernel,
        out_shape=jax.ShapeDtypeStruct((2, 1, SLOTS, block, everyone), BF16),
        in_specs=[vmem, vmem],
        out_specs=pl.BlockSpec(memory_space=pltpu.HBM),
        scratch_shapes=[
            pltpu.VMEM((2, SLOTS, block, everyone), BF16),
            pltpu.SemaphoreType.DMA((SLOTS * everyone // COLUMNS,)),
        ],
        compiler_params=pltpu.CompilerParams(vmem_limit_bytes=48 * 2**20),
        name="correlate",
    )(left, right)


def solution(mesh):
    n_band, n_blk = mesh.shape["band"], mesh.shape["blk"]

    def local(volt, band_chans, band_count):
        chans, count = (
            pltpu.with_memory_space_constraint(a, pltpu.HBM) for a in (band_chans, band_count)
        )
        left, right = front(volt, chans, count, n_band, n_blk)
        return correlate(left, right)

    return jax.shard_map(
        local,
        mesh=mesh,
        in_specs=(P(None, ("blk", "band"), None), P(), P()),
        out_specs=P(None, "band", None, "blk", None),
        check_vma=False,
    )
```

```python
import math

import jax
import jax.numpy as jnp
import numpy as np
from jax import lax
from jax.experimental import pallas as pl
from jax.experimental.pallas import tpu as pltpu
from jax.sharding import PartitionSpec as P

C = 4096
TAPS = 16
NSPEC = 12
FRAMES = NSPEC + TAPS - 1
EL = 16
LANES = 128
BANDS = 8
SLOTS = 8
GROUPS = 4
GROUP_W = C // GROUPS
CHUNK = 512
N_CENTRE = 2
N_CHUNK = C // CHUNK
MESH = pl.DeviceIdType.MESH
F32, BF16 = jnp.float32, jnp.bfloat16


def taper_scale():
    idx = np.arange(TAPS * C, dtype=np.float64)
    centre = (idx + 0.5) / C - TAPS / 2.0
    window = 0.5 - 0.5 * np.cos(2.0 * math.pi * (idx + 0.5) / (TAPS * C))
    prototype = np.sinc(centre) * window
    return float(1.0 / np.sqrt(np.sum(prototype * prototype)))


def half_sine(x):
    y = jnp.minimum(x, math.pi - x)
    y2 = y * y
    s = 1.0 / 120 + y2 * (-1.0 / 5040 + y2 * (1.0 / 362880 + y2 * (-1.0 / 39916800)))
    return y * (1.0 + y2 * (-1.0 / 6 + y2 * s))


def fill_taper(taper):
    width = 512
    scale = taper_scale() / math.pi

    def some(n, carry):
        tap = lax.broadcasted_iota(jnp.int32, (TAPS, width), 0)
        k = lax.broadcasted_iota(jnp.int32, (TAPS, width), 1) + n * width
        frac = (k.astype(F32) + 0.5) * (1.0 / C)
        top = half_sine(frac * math.pi) * jnp.where((tap & 1) == 0, scale, -scale)
        window = half_sine((tap.astype(F32) + frac) * (math.pi / TAPS))
        value = top * window * window / (frac + (tap - TAPS // 2).astype(F32))
        taper[:, pl.ds(pl.multiple_of(n * width, width), width)] = value
        return carry

    lax.fori_loop(0, C // width, some, 0)


def cos_sin(turns):
    shifted = turns + 512
    quarter = (shifted >> 10) & 3
    x = ((shifted & 1023) - 512).astype(F32) * (2.0 * math.pi / 4096.0)
    x2 = x * x
    s = x * (1.0 + x2 * (-1.0 / 6 + x2 * (1.0 / 120 + x2 * (-1.0 / 5040 + x2 * (1.0 / 362880)))))
    c = 1.0 + x2 * (-0.5 + x2 * (1.0 / 24 + x2 * (-1.0 / 720 + x2 * (1.0 / 40320))))
    odd = (quarter & 1) == 1
    cc, ss = jnp.where(odd, s, c), jnp.where(odd, c, s)
    cc = jnp.where((quarter == 1) | (quarter == 2), -cc, cc)
    ss = jnp.where(quarter >= 2, -ss, ss)
    return cc, ss


def split(y):
    hi = y.astype(BF16)
    return hi, (y - hi.astype(F32)).astype(BF16)


CENTRE = tuple(range(TAPS // 2 - N_CENTRE // 2, TAPS // 2 + N_CENTRE // 2))
OUTER = tuple(p for p in range(TAPS) if p not in CENTRE)
ROWS = 2 * NSPEC * EL


def front_kernel(
    n_band, n_blk, volt, chans_hbm, count_hbm, left, right, chans, count, taper, small_sem, samples, base_c, base_s,
    step_c, step_s, table, lhs_a, lhs_b, total, sems, z, turned, x, *comm_sems
):
    def fetch(group, frame):
        return pltpu.make_async_copy(
            volt.at[:, :, pl.ds(frame * C + group * GROUP_W, GROUP_W)],
            samples.at[group, frame],
            sems.at[group],
        )

    def fetch_group(group):
        for frame in range(FRAMES):
            fetch(group, frame).start()

    small = [
        pltpu.make_async_copy(chans_hbm, chans, small_sem.at[0]),
        pltpu.make_async_copy(count_hbm, count, small_sem.at[1]),
    ]
    for copy in small:
        copy.start()
    fetch_group(0)
    greet(n_band, n_blk)
    fetch_group(1)
    fill_taper(taper)
    for copy in small:
        copy.wait()

    lane = lax.broadcasted_iota(jnp.int32, (8, LANES), 1)
    key = ((lane >> 4) << 3) + (lane & 7)
    row = jnp.zeros((8, LANES), jnp.int32)
    for g in range(BANDS):
        for s in range(SLOTS):
            row = jnp.where(key == g * SLOTS + s, chans[g, s], row)
    quarter_turn = ((lane[:1] >> 3) & 1) * 1024
    row = row[:1]
    inner = lax.broadcasted_iota(jnp.int32, (LANES, LANES), 0)
    c0, s0 = cos_sin((inner * row + quarter_turn) & 4095)
    base_c[...] = c0
    base_s[...] = s0
    outer = lax.broadcasted_iota(jnp.int32, (C // LANES, LANES), 0) * LANES
    c1, s1 = cos_sin((outer * row) & 4095)
    step_c[...] = c1
    step_s[...] = s1

    def build(chunk, carry):
        for part in range(CHUNK // LANES):
            a = chunk * (CHUNK // LANES) + part
            ca, sa = step_c[pl.ds(a, 1), :], step_s[pl.ds(a, 1), :]
            hi, lo = split(ca * base_c[...] - sa * base_s[...])
            rows = slice(part * LANES, (part + 1) * LANES)
            table[chunk, rows, :LANES] = hi
            table[chunk, rows, LANES:] = lo
        return carry

    lax.fori_loop(0, N_CHUNK, build, 0)

    def weigh(chunk, lhs, before=None):
        group = chunk // (GROUP_W // CHUNK)
        for part in range(CHUNK // LANES):
            k = chunk * CHUNK + part * LANES
            in_group = k - group * GROUP_W
            taps = [
                jnp.broadcast_to(taper[p : p + 1, pl.ds(k, LANES)], (EL, LANES))
                for p in range(TAPS)
            ]
            taps = [taps[p] if p in CENTRE else taps[p].astype(BF16) for p in range(TAPS)]
            column = slice(part * LANES, (part + 1) * LANES)
            if before is not None:
                piece(before[0], before[1], part)
            for comp in range(2):
                x = [samples[group, f, comp, :, pl.ds(in_group, LANES)] for f in range(FRAMES)]
                for t in range(NSPEC):
                    sides = []
                    for order in (OUTER[: len(OUTER) // 2], OUTER[: len(OUTER) // 2 - 1 : -1]):
                        side = taps[order[0]] * x[t + order[0]]
                        for p in order[1:]:
                            side = side + taps[p] * x[t + p]
                        sides.append(side)
                    y = sides[0].astype(F32) + sides[1].astype(F32)
                    for p in CENTRE:
                        y = y + taps[p] * x[t + p].astype(F32)
                    hi, lo = split(y)
                    at = (comp * NSPEC + t) * EL
                    lhs[at : at + EL, column] = hi
                    lhs[ROWS + at : ROWS + at + EL, column] = lo

    def piece(chunk, lhs, n):
        count = ROWS // 2
        at = n * count
        if n < 2:
            r = jnp.dot(lhs[at : at + count, :], table[chunk], preferred_element_type=F32)
            total[at : at + count, :] += r[:, :LANES] + r[:, LANES:]
        else:
            r = jnp.dot(lhs[at : at + count, :], table[chunk, :, :LANES], preferred_element_type=F32)
            total[at - ROWS : at - ROWS + count, :] += r

    def wait_group(group):
        pltpu.make_async_copy(samples.at[group], samples.at[group], sems.at[group]).wait()

    total[...] = jnp.zeros_like(total)
    per_group = GROUP_W // CHUNK
    held, other, before = lhs_a, lhs_b, None
    for chunk in range(N_CHUNK):
        if chunk % per_group == 0:
            group = chunk // per_group
            if group + 2 < GROUPS:
                fetch_group(group + 2)
            wait_group(group)
        weigh(chunk, held, before)
        before = (chunk, held)
        held, other = other, held
    for n in range(4):
        piece(*before, n)

    is_real = (lax.broadcasted_iota(jnp.int32, (EL, LANES), 1) & 8) == 0
    y = []
    for t in range(NSPEC):
        re = total[t * EL : (t + 1) * EL, :]
        im = total[(NSPEC + t) * EL : (NSPEC + t + 1) * EL, :]
        swapped = jnp.where(is_real, -pltpu.roll(im, LANES - 8, 1), pltpu.roll(im, 8, 1))
        y.append(re + swapped)
    place = lax.broadcasted_iota(jnp.int32, (EL, LANES), 1) >> 4
    for g in range(BANDS):
        for tile in range(2):
            out = jnp.zeros((EL, LANES), F32)
            for t in range(tile * 8, min(tile * 8 + 8, NSPEC)):
                moved = y[t]
                shift = (t - g) * 16 % LANES
                if shift:
                    moved = pltpu.roll(moved, shift, 1)
                out = jnp.where(place == t - tile * 8, moved, out)
            z[g, :, tile * LANES : (tile + 1) * LANES] = out.astype(BF16)
    share(n_band, n_blk, z, turned, x, count, left, right, *comm_sems)


def places(n_band, n_blk):
    g, b = lax.axis_index("band"), lax.axis_index("blk")
    core, near, along = b % 2, b // 2 % 2, b // 4
    n_along = n_blk // 4

    def chip(d_along, d_near):
        return ((along + d_along + n_along) % n_along * 2 + (near + d_near) % 2) * 2 + core

    return g, b, b + 1 - 2 * core, chip


STEPS = ((1, 0), (-1, 1), (-1, 0), (1, 1), (0, 1))
PASSED = (0, 1)


NEARBY = ((0, 0), (0, 1), (1, 0), (1, 1), (-1, 0), (-1, 1), (2, 0), (2, 1))


def slot_of(d_along, d_near):
    return NEARBY.index(((d_along + 1) % 4 - 1, d_near))


PACKED = 192


def greet(n_band, n_blk):
    g, b, sibling, chip = places(n_band, n_blk)
    peers = [((g + d) % n_band, b) for d in range(1, n_band)]
    peers += [(g, chip(*step)) for step in STEPS] + [(g, sibling)]
    peers += [(g, chip(da, 0) + sibling - b) for da in (1, -1)]
    barrier = pltpu.get_barrier_semaphore()
    for peer in peers:
        pl.semaphore_signal(barrier, inc=1, device_id=peer, device_id_type=MESH)


def fill_left(left, turned, live):
    block = turned.shape[0]
    for tile in range(2):
        cols = slice(tile * LANES, (tile + 1) * LANES)
        own = turned[:, cols].astype(F32)
        lane = lax.broadcasted_iota(jnp.int32, own.shape, 1)
        slot = lane & 7
        crossed = jnp.where(
            (lane & 8) == 0, pltpu.roll(own, LANES - 8, 1), -pltpu.roll(own, 8, 1)
        )
        own, crossed = jnp.where(slot < live, own, 0.0), jnp.where(slot < live, crossed, 0.0)
        for s in range(SLOTS):
            for part, value in ((0, own), (1, crossed)):
                at = (part * SLOTS + s) * block
                left[at : at + block, cols] = jnp.where(slot == s, value, 0.0).astype(BF16)


def share(
    n_band, n_blk, z, turned, x, count, left, right, ct_send, ct_recv, ag_send, ag_recv, fw_send,
    fw_recv, here,
):
    g, b, sibling, chip = places(n_band, n_blk)
    pl.semaphore_wait(pltpu.get_barrier_semaphore(), n_band - 1 + len(STEPS) + 3)
    block = EL * n_band
    half = block // 2
    core = b % 2
    low = lax.broadcasted_iota(jnp.int32, (half, LANES), 1) < LANES // 2

    def slots(of_core, start, count=1):
        at = pl.multiple_of((of_core * (n_blk // 2) + start) * PACKED, PACKED)
        return x.at[pl.ds(at, count * PACKED)]

    def remote(src, dst, send, recv, to):
        copy = pltpu.make_async_remote_copy(src, dst, send, recv, to, MESH)
        copy.start()
        return copy

    def unpack(of_core, first, count):
        for slot in range(first, first + count):
            owner = chip(*NEARBY[slot]) - core + of_core
            at = pl.multiple_of(owner * block, block)
            kept = slots(of_core, slot)
            right[pl.ds(at, block), :LANES] = kept[:block, :]
            packed = kept[block:, :].astype(F32)
            for n, part in enumerate((packed, pltpu.roll(packed, LANES // 2, 1))):
                part = jnp.where(low, part, 0.0).astype(BF16)
                right[pl.ds(pl.multiple_of(at + n * half, half), half), LANES:] = part

    mine = turned.at[pl.ds(pl.multiple_of(g * EL, EL), EL)]
    turns = []
    for d in range(1, n_band):
        to = (g + d) % n_band
        turns.append(remote(z.at[to], mine, ct_send.at[d], ct_recv.at[d], (to, b)))
    keep = pltpu.make_async_copy(z.at[g], mine, here.at[0])
    keep.start()
    keep.wait()
    for turn in turns:
        turn.wait_recv()
    own = slots(core, 0)
    top = turned[:half, LANES:].astype(F32)
    bottom = pltpu.roll(turned[half:, LANES:].astype(F32), LANES // 2, 1)
    own[:block, :] = turned[:, :LANES]
    own[block:, :] = jnp.where(low, top, bottom).astype(BF16)

    sends = [
        remote(own, slots(core, slot_of(-da, dn)), ag_send.at[n], ag_recv.at[n], (g, chip(da, dn)))
        for n, (da, dn) in enumerate(STEPS)
    ]
    fill_left(left, turned, count[g])
    unpack(core, 0, 1)
    onward = []
    for n, (da, dn) in enumerate(STEPS):
        sends[n].wait_recv()
        if n in PASSED:
            m = len(STEPS) + len(onward)
            came, goes = slots(core, slot_of(-da, dn)), slots(core, slot_of(-2 * da, dn))
            for n_core, to in enumerate((chip(da, 0), chip(da, 0) + 1 - 2 * core)):
                onward.append(
                    remote(came, goes, ag_send.at[m + n_core], ag_recv.at[m + n_core], (g, to))
                )
    n_near = len(STEPS) + 1
    near = slots(core, 0, n_near)
    near_copy = remote(near, near, fw_send.at[0], fw_recv.at[0], (g, sibling))
    unpack(core, 1, n_near - 1)
    near_copy.wait_recv()
    unpack(1 - core, 0, n_near)
    for copy in onward:
        copy.wait_recv()
    unpack(core, n_near, 2)
    unpack(1 - core, n_near, 2)
    for copy in turns + sends + onward + [near_copy]:
        copy.wait_send()


def front(volt, chans, count, n_band, n_blk):
    hbm = pl.BlockSpec(memory_space=pltpu.HBM)
    dma = pltpu.SemaphoreType.DMA
    n_copies = len(STEPS) + 2 * len(PASSED)
    vmem = pl.BlockSpec(memory_space=pltpu.VMEM)

    def body(*refs):
        front_kernel(n_band, n_blk, *refs)

    return pl.pallas_call(
        body,
        out_shape=[
            jax.ShapeDtypeStruct((2 * SLOTS * EL * n_band, 2 * LANES), BF16),
            jax.ShapeDtypeStruct((EL * n_band * n_blk, 2 * LANES), BF16),
        ],
        in_specs=[hbm] * 3,
        out_specs=[vmem] * 2,
        scratch_shapes=[
            pltpu.SMEM((BANDS, SLOTS), jnp.int32),
            pltpu.SMEM((BANDS,), jnp.int32),
            pltpu.VMEM((TAPS, C), F32),
            dma((2,)),
            pltpu.VMEM((GROUPS, FRAMES, 2, EL, GROUP_W), BF16),
            pltpu.VMEM((LANES, LANES), F32),
            pltpu.VMEM((LANES, LANES), F32),
            pltpu.VMEM((C // LANES, LANES), F32),
            pltpu.VMEM((C // LANES, LANES), F32),
            pltpu.VMEM((N_CHUNK, CHUNK, 2 * LANES), BF16),
            pltpu.VMEM((2 * ROWS, CHUNK), BF16),
            pltpu.VMEM((2 * ROWS, CHUNK), BF16),
            pltpu.VMEM((ROWS, LANES), F32),
            dma((GROUPS,)),
            pltpu.VMEM((BANDS, EL, 2 * LANES), BF16),
            pltpu.VMEM((EL * n_band, 2 * LANES), BF16),
            pltpu.VMEM((n_blk * PACKED, LANES), BF16),
            dma((n_band,)),
            dma((n_band,)),
            dma((n_copies,)),
            dma((n_copies,)),
            dma((2,)),
            dma((2,)),
            dma((1,)),
        ],
        compiler_params=pltpu.CompilerParams(
            vmem_limit_bytes=48 * 2**20, collective_id=0, has_side_effects=True
        ),
        name="spectra",
    )(volt, chans, count)


COLUMNS = 512


def correlate_kernel(left, right, out, done, sems):
    block = out.shape[3]
    everyone = right.shape[0]
    copies = []
    for at in range(0, everyone, COLUMNS):
        cols = slice(at, at + COLUMNS)
        for first, last in ((0, 4), (4, 8), (8, 16)) if at == 0 else ((0, 8), (8, 16)):
            y = lax.dot_general(
                left[first * block : last * block, :],
                right[cols, :],
                (((1,), (1,)), ((), ())),
                preferred_element_type=F32,
            )
            y = (y * (1.0 / NSPEC)).astype(BF16)
            for n in range(first, last):
                part, s = n // SLOTS, n % SLOTS
                done[part, s, :, cols] = y[(n - first) * block : (n - first + 1) * block]
                if n % 2:
                    pair = pl.ds(s - 1, 2)
                    copies.append(
                        pltpu.make_async_copy(
                            done.at[part, pair, :, pl.ds(at, COLUMNS)],
                            out.at[part, 0, pair, :, pl.ds(at, COLUMNS)],
                            sems.at[len(copies)],
                        )
                    )
                    copies[-1].start()
    for copy in copies:
        copy.wait()


def correlate(left, right):
    block, everyone = left.shape[0] // (2 * SLOTS), right.shape[0]
    vmem = pl.BlockSpec(memory_space=pltpu.VMEM)
    return pl.pallas_call(
        correlate_kernel,
        out_shape=jax.ShapeDtypeStruct((2, 1, SLOTS, block, everyone), BF16),
        in_specs=[vmem, vmem],
        out_specs=pl.BlockSpec(memory_space=pltpu.HBM),
        scratch_shapes=[
            pltpu.VMEM((2, SLOTS, block, everyone), BF16),
            pltpu.SemaphoreType.DMA((SLOTS * everyone // COLUMNS,)),
        ],
        compiler_params=pltpu.CompilerParams(vmem_limit_bytes=48 * 2**20),
        name="correlate",
    )(left, right)


def solution(mesh):
    n_band, n_blk = mesh.shape["band"], mesh.shape["blk"]

    def local(volt, band_chans, band_count):
        chans, count = (
            pltpu.with_memory_space_constraint(a, pltpu.HBM) for a in (band_chans, band_count)
        )
        left, right = front(volt, chans, count, n_band, n_blk)
        return correlate(left, right)

    return jax.shard_map(
        local,
        mesh=mesh,
        in_specs=(P(None, ("blk", "band"), None), P(), P()),
        out_specs=P(None, "band", None, "blk", None),
        check_vma=False,
    )
```
